32 devices in a mesh: groups: 2 (over x), row: 16 (over z, y, core).
Axes of the slice: x: 2, y: 2, z: 4, core: 2. Of those that a mesh axis runs over, the one named last changes fastest.
Arguments:
- inputs: bfloat16 [1024, 8192], P(('groups', 'row')), parts along dimension 0, may hold values from -6 to 6
- input_factor: bfloat16 [16384, 8192], P(('groups', 'row')), parts along dimension 0, as said below
- out_grads: bfloat16 [1024, 16384], P(('groups', 'row')), parts along dimension 0, may hold values from -6 to 6
- output_factor: float32 [32768, 4096], P(('groups', 'row')), parts along dimension 0, may hold values from -6 to 6
Outputs:
- updated_factor: float32 [32768, 4096], P(('groups', 'row')), parts along dimension 0
The draws below stay inside these ranges and needn't reach their ends.
There are 2 independent parts, one for each index of `groups`. The reference program is written for one: setup_inputs(seed, part) draws one part's arguments, and reference() takes and returns one part's arrays. A program takes and returns all parts, laid end to end along the dimension named above; each array names one. Nothing has to cross between parts.
Inputs may be any that keep to these rules, and one draw needn't show every extreme that they name: input_factor is symmetric.
All inputs are finite; a program needn't handle non-finite values.
Results may differ from the reference program's by a relative error of at most 0.0041.
Values may be sent and summed in bfloat16 or wider, within the bound.
A program may use at most 192 MiB of HBM per device.

```python
import jax
import jax.numpy as jnp

DIN = 8192
DOUT = 16384
SLAB = 4096
TOKENS = 512
N_ROW = 16


def draw_input_factor(key, part):
    base = jax.random.truncated_normal(key, -4.0, 4.0, (DIN, DIN), jnp.float32)
    symmetric = (base + base.T) * 0.5 ** 0.5
    width = DIN // N_ROW
    row_block = jnp.arange(DIN, dtype=jnp.int32) // width
    same_block = (row_block[:, None] == row_block[None, :]).astype(jnp.float32)
    boosted = symmetric * (1.0 + 2.0 * same_block)
    return (boosted * float(DIN) ** (-0.5)).astype(jnp.bfloat16)


def block_scale(key, shape, split, low, high):
    def one(position, parts):
        draws = jax.random.uniform(jax.random.fold_in(jax.random.fold_in(key, 6), position), (parts,), jnp.float32, low / len(split), high / len(split))
        return jnp.repeat(jnp.exp(draws), shape[position] // parts).reshape((-1,) + (1,) * (len(shape) - position - 1))

    factor_of = one(*split[0])
    for cut in split[1:]:
        factor_of = factor_of * one(*cut)
    return factor_of


def scatter_about(rng, dims, scale, reach, cuts=(), kind=jnp.bfloat16):
    level = block_scale(rng, dims, cuts, -0.22, 0.18) if cuts else 1.0
    values = jax.random.normal(rng, dims, jnp.float32) * scale * level
    return jnp.minimum(jnp.maximum(values, -reach), reach).astype(kind)


def setup_inputs(seed: int = 0, part: int = 0) -> dict:
    splits = jax.random.split(jax.random.key(seed), 5)
    own_keys = jax.random.split(jax.random.fold_in(splits[4], part), 5)
    return {
        "inputs": scatter_about(own_keys[0], (TOKENS, DIN), 1.0, 6.0, ((0, 16),)),
        "input_factor": draw_input_factor(jax.random.fold_in(jax.random.fold_in(splits[4], part), 71), part),
        "out_grads": scatter_about(own_keys[2], (TOKENS, DOUT), 1.0, 6.0, ((0, 16),)),
        "output_factor": scatter_about(own_keys[3], (DOUT, SLAB), 1.0, 6.0, ((0, 16),), jnp.float32),
    }


def reference(inputs, input_factor, out_grads, output_factor):
    projected = jnp.dot(inputs, input_factor, preferred_element_type=jnp.float32).astype(jnp.bfloat16)
    summed = jnp.dot(projected, inputs.T, preferred_element_type=jnp.float32)
    gram = (summed * (float(DIN) ** -0.5)).astype(jnp.bfloat16)
    left = jnp.dot(out_grads.T, gram, preferred_element_type=jnp.float32).astype(jnp.bfloat16)
    update = jnp.dot(left, out_grads[:, :SLAB], preferred_element_type=jnp.float32)
    return output_factor + update * (1.0 / TOKENS)
```

```python
import functools

import jax
import jax.numpy as jnp
from jax import lax
from jax.experimental import pallas as pl
from jax.experimental.pallas import tpu as pltpu
from jax.sharding import PartitionSpec as P

UP, DOWN, SIDE, CORE = range(4)
CHUNKS = 4


def exchange_kernel(
    n, x_ref, f_ref, g_ref, of_ref, upd_ref,
    xall, fv, gv, slab_ref, cols_ref, proj, proj_low, part, out0, in0, out1, in1, out2, in2, final,
    local_sem, x_recv, x_send, s_recv, s_send, c_recv, c_send,
    r_recv, r_send, z2_recv, z2_send, z3_recv, z3_send,
):
    me = lax.axis_index("row")
    depth = n // 4
    z, y, c = me // 4, (me // 2) % 2, me % 2
    sh = x_ref.shape[0]
    tokens = n * sh
    slab = slab_ref.shape[1]
    width = cols_ref.shape[1]
    part_width = width // CHUNKS
    feat = f_ref.shape[0]
    chips = n // 2
    chip = z * 2 + y
    half_way = chips // 2

    def index(zz, yy, cc):
        return zz * 4 + yy * 2 + cc

    side, peer = index(z, 1 - y, c), index(z, y, 1 - c)

    def rows(start, size):
        return pl.ds(pl.multiple_of(start, size), size)

    def is_end(zz):
        return (zz == 0) | (zz == depth - 1)

    load_f = pltpu.make_async_copy(f_ref, fv, local_sem.at[0])
    load_x = pltpu.make_async_copy(x_ref, xall.at[rows(me * sh, sh), :], local_sem.at[1])
    load_g = pltpu.make_async_copy(g_ref, gv, local_sem.at[2])
    load_of = pltpu.make_async_copy(of_ref, upd_ref, local_sem.at[5])
    load_x.start()
    load_g.start()
    load_f.start()

    barrier = pltpu.get_barrier_semaphore()
    for k in range(1, n):
        pl.semaphore_signal(
            barrier, inc=1, device_id={"row": (me + k) % n}, device_id_type=pl.DeviceIdType.MESH
        )
    pl.semaphore_wait(barrier, n - 1)

    def send(src, dst, send_sem, recv_sem, target):
        return pltpu.make_async_remote_copy(
            src_ref=src, dst_ref=dst, send_sem=send_sem, recv_sem=recv_sem,
            device_id={"row": target}, device_id_type=pl.DeviceIdType.MESH,
        )

    class Gather:
        def __init__(self, buf, recv, sems, pieces, groups, windowed):
            self.buf, self.recv, self.sems = buf, recv, sems
            self.pieces, self.groups, self.windowed = pieces, groups, windowed
            self.width = buf.shape[1] // pieces
            self.size = pieces // groups
            self.end_near = half_way if windowed else pieces
            self.mid_near = min(half_way + 1, pieces) if windowed else pieces
            self.end_along = min(self.end_near + 1, pieces) if windowed else pieces

        def along_takes(self, zz, p):
            if not self.windowed:
                return True
            return jnp.logical_not(is_end(zz)) | ((p - 2 * zz + self.pieces) % self.pieces < self.end_along)

        def near_takes(self, cc, p):
            if not self.windowed:
                return True
            reach = jnp.where(is_end(z), self.end_near, self.mid_near)
            return (p - cc + self.pieces) % self.pieces < reach

        def copy(self, origin, kind, target, first, count, group, src=None):
            cols = pl.ds(pl.multiple_of(first * self.width, self.width), count * self.width)
            view = self.buf.at[rows(origin * sh, sh), cols]
            return send(
                view if src is None else src.at[:, cols], view,
                self.sems.at[kind, origin], self.recv.at[origin, group], target,
            )

        def when(self, gate, fn):
            if gate is True:
                fn()
            else:
                pl.when(gate)(fn)

        def along(self, origin, kind, group, src=None):
            to = z + 1 if kind == UP else z - 1
            for i in range(self.size):
                p = group * self.size + i
                self.when(self.along_takes(to, p), lambda: self.copy(
                    origin, kind, index(to, y, c), p, 1, group, src).start())

        def near_by(self, origin, group, src=None):
            for i in range(self.size):
                p = group * self.size + i
                self.when(self.near_takes(z * 2 + 1 - y, p), lambda: self.copy(
                    origin, SIDE, side, p, 1, 0, src).start())
                self.when(self.near_takes(chip, p), lambda: self.copy(
                    origin, CORE, peer, p, 1, 0, src).start())

        def each(self, fn):
            if self.groups == 1:
                fn(0)
            else:
                pl.loop(0, self.groups)(fn)

        def own_along(self, src=None):
            def go(group):
                @pl.when(z + 1 < depth)
                def _():
                    self.along(me, UP, group, src)

                @pl.when(z > 0)
                def _():
                    self.along(me, DOWN, group, src)

            self.each(go)

        def own_near(self, src=None):
            self.each(lambda group: self.near_by(me, group, src))

        def came(self, origin, group):
            def take(count):
                self.copy(origin, CORE, peer, 0, count, group).wait_recv()

            if not self.windowed:
                take(self.size)
                return
            got = sum(
                self.along_takes(z, group * self.size + i).astype(jnp.int32) for i in range(self.size)
            )
            for count in range(1, self.size + 1):
                pl.when(got == count)(functools.partial(take, count))

        def column(self, k, near=True):
            def go(group):
                @pl.when(z - k >= 0)
                def _():
                    origin = index(z - k, y, c)
                    self.came(origin, group)

                    @pl.when(z + 1 < depth)
                    def _():
                        self.along(origin, UP, group)

                    if near:
                        self.near_by(origin, group)

                @pl.when(z + k < depth)
                def _():
                    origin = index(z + k, y, c)
                    self.came(origin, group)

                    @pl.when(z > 0)
                    def _():
                        self.along(origin, DOWN, group)

                    if near:
                        self.near_by(origin, group)

            self.each(go)

        def column_near(self, k):
            def go(group):
                @pl.when(z - k >= 0)
                def _():
                    self.near_by(index(z - k, y, c), group)

                @pl.when(z + k < depth)
                def _():
                    self.near_by(index(z + k, y, c), group)

            self.each(go)

        def by_end(self, fn):
            if self.end_near == self.mid_near:
                fn(self.end_near)
            else:
                pl.when(is_end(z))(functools.partial(fn, self.end_near))
                pl.when(jnp.logical_not(is_end(z)))(functools.partial(fn, self.mid_near))

        def across(self, plane):
            origin = index(plane, 1 - y, c)
            self.by_end(lambda count: self.copy(origin, CORE, peer, 0, count, 0).wait_recv())

            def go(group):
                for i in range(self.size):
                    p = group * self.size + i
                    self.when(self.near_takes(chip, p), lambda: self.copy(
                        origin, CORE, peer, p, 1, 0).start())

            self.each(go)

        def whole(self, plane):
            def take(count):
                self.copy(index(plane, 0, 1 - c), CORE, peer, 0, count, 0).wait_recv()
                self.copy(index(plane, 1, 1 - c), CORE, peer, 0, count, 0).wait_recv()

            self.by_end(take)

        def drain(self):
            def sent(origin, kind, count):
                self.copy(origin, kind, peer, 0, count, 0).wait_send()

            for plane in range(depth):
                origin = index(plane, y, c)
                for kind, to, gate in (
                    (UP, z + 1, (plane <= z) & (z + 1 < depth)),
                    (DOWN, z - 1, (plane >= z) & (z > 0)),
                ):
                    if self.end_along == self.pieces:
                        pl.when(gate)(functools.partial(sent, origin, kind, self.pieces))
                    else:
                        pl.when(gate & is_end(to))(functools.partial(sent, origin, kind, self.end_along))
                        pl.when(gate & jnp.logical_not(is_end(to)))(
                            functools.partial(sent, origin, kind, self.pieces))

                def near(count, origin=origin, plane=plane):
                    sent(origin, SIDE, count)
                    sent(origin, CORE, count)
                    sent(index(plane, 1 - y, c), CORE, count)

                self.by_end(near)

    gx = Gather(xall, x_recv, x_send, chips, 4, True)
    gs = Gather(slab_ref, s_recv, s_send, 2, 2, False)
    gx.own_along(x_ref)
    gx.own_near(x_ref)

    flip = z >= (depth + 1) // 2
    zm = jnp.where(flip, depth - 1 - z, z)

    def plane_at(t):
        near = zm - (t + 1) // 2 if t % 2 else zm + t // 2
        p = jnp.where(t <= 2 * zm, near, t)
        return jnp.where(flip, depth - 1 - p, p)

    block = 4 * sh
    tile = min(256, feat)
    far = (z + depth // 2) % depth
    far_weight = jnp.where(is_end(far), 1.0, 0.5).astype(jnp.float32)

    def project(plane):
        xs = rows(plane * block, block)

        def body(reach):
            @pl.loop(0, feat // tile)
            def _(j):
                fs = rows(j * tile, tile)
                value = jnp.zeros((block, tile), jnp.float32)
                for k in range(reach):
                    cs = rows((chip + k) % chips * (2 * feat), 2 * feat)
                    term = lax.dot_general(
                        xall[xs, cs], fv[fs, cs], (((1,), (1,)), ((), ())),
                        preferred_element_type=jnp.float32,
                    )
                    if k == 0:
                        term = term * 0.5
                    elif k == half_way:
                        term = term * far_weight
                    value = value + term
                high = value.astype(jnp.bfloat16)
                proj[xs, fs] = high
                proj_low[xs, fs] = (value - high.astype(jnp.float32)).astype(jnp.bfloat16)

        gx.by_end(body)

    def cols_copy(d, origin, r):
        return send(
            gv.at[:, rows(d * width + r * part_width, part_width)],
            cols_ref.at[rows(origin * sh, sh), pl.ds(r * part_width, part_width)],
            c_send.at[r, d], c_recv.at[r, origin], d,
        )

    def send_cols(r):
        @pl.loop(1, n)
        def _(k):
            d = (me + k * 5) % n if n % 5 else (me + k) % n
            cols_copy(d, me, r).start()

    load_x.wait()
    load_g.wait()
    own_slab = pltpu.make_async_copy(
        gv.at[:, pl.ds(0, slab)], slab_ref.at[rows(me * sh, sh), :], local_sem.at[3]
    )
    own_cols = pltpu.make_async_copy(
        gv.at[:, rows(me * width, width)], cols_ref.at[rows(me * sh, sh), :], local_sem.at[4]
    )
    own_slab.start()
    own_cols.start()
    load_f.wait()
    load_of.start()

    slab_src = gv.at[:, pl.ds(0, slab)]
    for k in range(1, depth):
        gx.column(k)
        if k == max(1, depth - 2):
            gs.own_along(slab_src)
        if k == depth - 1:
            gs.own_near(slab_src)
            gs.column(1, near=False)
            send_cols(0)
        plane = plane_at(k - 1)
        gx.across(plane)
        gx.whole(plane)
        project(plane)
    plane = plane_at(depth - 1)
    gx.across(plane)
    gx.whole(plane)
    project(plane)

    own_features = rows(me * feat, feat)
    half, quarter = tokens // 2, tokens // 4

    def partial_rows(start, size):
        some = rows(start, size)
        total = jnp.zeros((size, tokens), jnp.float32)
        for piece in (proj, proj_low):
            for left, right in ((piece[some, :], xall[:, own_features]), (xall[some, own_features], piece[...])):
                total = total + lax.dot_general(
                    left, right, (((1,), (1,)), ((), ())), preferred_element_type=jnp.float32
                )
        return total

    out0[...] = partial_rows((1 - c) * half, half)
    core_sum = send(out0, in0, r_send.at[0], r_recv.at[0], peer)
    core_sum.start()
    part[...] = partial_rows(c * half, half)
    core_sum.wait_recv()
    gone, kept = rows((1 - y) * quarter, quarter), rows(y * quarter, quarter)
    out1[...] = (part[gone, :] + in0[gone, :]).astype(jnp.bfloat16)
    side_sum = send(out1, in1, r_send.at[1], r_recv.at[1], side)
    side_sum.start()
    part[kept, :] = part[kept, :] + in0[kept, :]
    gs.column_near(1)
    for k in range(2, depth):
        gs.column(k)
        if k == 2:
            send_cols(1)
    side_sum.wait_recv()
    part[kept, :] = part[kept, :] + in1[...].astype(jnp.float32)
    out2[...] = part[kept, :].astype(jnp.bfloat16)

    def z_sum(k):
        zz = (z + k) % depth
        return send(
            out2.at[rows(zz * sh, sh), :], in2.at[k], z2_send.at[k], z2_recv.at[k], index(zz, y, c)
        )

    for k in range(1, depth):
        z_sum(k).start()
    send_cols(2)
    for t in range(depth // 2):
        gs.across(plane_at(t))
    total = part[rows(y * quarter + z * sh, sh), :]
    for k in range(1, depth):
        z_sum(k).wait_recv()
        total = total + in2[k].astype(jnp.float32)
    scale = float(n * feat) ** (-0.5)
    base = c * half + y * quarter
    mine = rows(base + z * sh, sh)
    final[mine, :] = (total * scale).astype(jnp.bfloat16)

    def z_spread(k):
        zz = (z + k) % depth
        return send(
            final.at[mine, :], final.at[mine, :], z3_send.at[k], z3_recv.at[k], index(zz, y, c)
        )

    for k in range(1, depth):
        z_spread(k).start()
    for k in range(1, depth):
        z_spread(k).wait_recv()
    view = final.at[rows(base, quarter), :]
    side_spread = send(view, view, r_send.at[2], r_recv.at[2], side)
    side_spread.start()
    send_cols(3)
    for t in range(depth // 2, depth):
        gs.across(plane_at(t))
    side_spread.wait_recv()
    view = final.at[rows(c * half, half), :]
    core_spread = send(view, view, r_send.at[3], r_recv.at[3], peer)
    core_spread.start()
    core_spread.wait_recv()
    for t in range(depth):
        gs.whole(plane_at(t))
    own_slab.wait()
    own_cols.wait()
    load_of.wait()

    strip = min(512, slab)
    for r in range(CHUNKS):
        for k in range(1, n):
            cols_copy(me, (me + k) % n, r).wait_recv()
        left = lax.dot_general(
            cols_ref[:, pl.ds(r * part_width, part_width)], final[...], (((0,), (0,)), ((), ())),
            preferred_element_type=jnp.float32,
        ).astype(jnp.bfloat16)
        some = pl.ds(r * part_width, part_width)

        @pl.loop(0, slab // strip)
        def _(j):
            cs = rows(j * strip, strip)
            upd_ref[some, cs] = upd_ref[some, cs] + jnp.dot(
                left, slab_ref[:, cs], preferred_element_type=jnp.float32
            ) * (1.0 / tokens)

    gx.drain()
    gs.drain()
    for r in range(CHUNKS):
        for k in range(1, n):
            cols_copy((me + k) % n, me, r).wait_send()
    for copy in (core_sum, side_sum, side_spread, core_spread):
        copy.wait_send()
    for k in range(1, depth):
        z_sum(k).wait_send()
        z_spread(k).wait_send()


def exchange(n, x, f, g, of):
    sh, din = x.shape
    feat = f.shape[0]
    tokens, depth = n * sh, n // 4
    width, slab = g.shape[1] // n, of.shape[1]
    half, quarter = tokens // 2, tokens // 4
    bf, f32, dma = jnp.bfloat16, jnp.float32, pltpu.SemaphoreType.DMA
    scratch = [
        ((tokens, din), bf), (f.shape, bf), (g.shape, bf), ((tokens, slab), bf), ((tokens, width), bf),
        ((tokens, feat), bf), ((tokens, feat), bf),
        ((half, tokens), f32), ((half, tokens), f32), ((half, tokens), f32),
        ((quarter, tokens), bf), ((quarter, tokens), bf), ((quarter, tokens), bf),
        ((depth, sh, tokens), bf), ((tokens, tokens), bf),
    ]
    used = sum(functools.reduce(lambda a, b: a * b, s) * jnp.dtype(t).itemsize for s, t in scratch)
    return pl.pallas_call(
        functools.partial(exchange_kernel, n),
        out_shape=pltpu.VMEM(of.shape, of.dtype),
        in_specs=[pl.BlockSpec(memory_space=pltpu.HBM)] * 4,
        out_specs=pl.BlockSpec(memory_space=pltpu.VMEM),
        scratch_shapes=[pltpu.VMEM(s, t) for s, t in scratch] + [
            dma((6,)), dma((n, 4)), dma((4, n)), dma((n, 2)), dma((4, n)),
            dma((CHUNKS, n)), dma((CHUNKS, n)), dma((4,)), dma((4,)),
            dma((depth,)), dma((depth,)), dma((depth,)), dma((depth,)),
        ],
        compiler_params=pltpu.CompilerParams(
            collective_id=0, has_side_effects=True, vmem_limit_bytes=used + 6 * 1024 * 1024
        ),
    )(*(pltpu.with_memory_space_constraint(v, pltpu.HBM) for v in (x, f, g, of)))


def write_kernel(src, dst, sem):
    size = src.shape[0] // sem.shape[0]

    def copy(i):
        some = pl.ds(i * size, size)
        return pltpu.make_async_copy(src.at[some, :], dst.at[some, :], sem.at[i])

    for i in range(sem.shape[0]):
        copy(i).start()
    for i in range(sem.shape[0]):
        copy(i).wait()


def write(x):
    return pl.pallas_call(
        write_kernel,
        out_shape=jax.ShapeDtypeStruct(x.shape, x.dtype),
        in_specs=[pl.BlockSpec(memory_space=pltpu.VMEM)],
        out_specs=pl.BlockSpec(memory_space=pl.ANY),
        scratch_shapes=[pltpu.SemaphoreType.DMA((8,))],
        compiler_params=pltpu.CompilerParams(vmem_limit_bytes=1024 * 1024),
    )(x)


def per_device(n, inputs, input_factor, out_grads, output_factor):
    return write(exchange(n, inputs, input_factor, out_grads, output_factor))


def solution(mesh):
    spec = P(("groups", "row"), None)
    return jax.shard_map(
        functools.partial(per_device, mesh.shape["row"]),
        mesh=mesh, in_specs=(spec,) * 4, out_specs=spec, check_vma=False,
    )
```

```python
import functools

import jax
import jax.numpy as jnp
from jax import lax
from jax.experimental import pallas as pl
from jax.experimental.pallas import tpu as pltpu
from jax.sharding import PartitionSpec as P

UP, DOWN, SIDE, CORE = range(4)
BLOCKS = 4
PACKED = BLOCKS * (BLOCKS + 1) // 2
SPLIT = ((0, 2), (2, 2))
UNITS = 4


def exchange_kernel(
    n, x_ref, f_ref, g_ref, of_ref, upd_ref, slab_ref, left_ref,
    xall, fv, gv, cols_ref, proj, proj_low, part, in0, out1, in1, packed, final,
    local_sem, x_recv, x_send, s_recv, s_send, c_recv, c_send,
    r_recv, r_send, rs_recv, rs_send, ag_recv, ag_send,
):
    me = lax.axis_index("row")
    depth = n // 4
    z, y, c = me // 4, (me // 2) % 2, me % 2
    sh = x_ref.shape[0]
    tokens = n * sh
    slab = slab_ref.shape[1]
    width = cols_ref.shape[1]
    unit = width // UNITS
    feat = f_ref.shape[0]
    chips = n // 2
    chip = z * 2 + y
    half_way = chips // 2

    def index(zz, yy, cc):
        return zz * 4 + yy * 2 + cc

    side, peer = index(z, 1 - y, c), index(z, y, 1 - c)

    def rows(start, size):
        return pl.ds(pl.multiple_of(start, size), size)

    def is_end(zz):
        return (zz == 0) | (zz == depth - 1)

    load_f = pltpu.make_async_copy(f_ref, fv, local_sem.at[0])
    load_x = pltpu.make_async_copy(x_ref, xall.at[rows(me * sh, sh), :], local_sem.at[1])
    load_g = pltpu.make_async_copy(g_ref, gv, local_sem.at[2])
    load_of = pltpu.make_async_copy(of_ref, upd_ref, local_sem.at[5])
    load_x.start()
    load_g.start()
    load_f.start()

    barrier = pltpu.get_barrier_semaphore()
    for k in range(1, n):
        pl.semaphore_signal(
            barrier, inc=1, device_id={"row": (me + k) % n}, device_id_type=pl.DeviceIdType.MESH
        )
    pl.semaphore_wait(barrier, n - 1)

    def send(src, dst, send_sem, recv_sem, target):
        return pltpu.make_async_remote_copy(
            src_ref=src, dst_ref=dst, send_sem=send_sem, recv_sem=recv_sem,
            device_id={"row": target}, device_id_type=pl.DeviceIdType.MESH,
        )

    class Gather:
        def __init__(self, buf, recv, sems, pieces, groups, windowed):
            self.buf, self.recv, self.sems = buf, recv, sems
            self.pieces, self.groups, self.windowed = pieces, groups, windowed
            self.width = buf.shape[1] // pieces
            self.size = pieces // groups
            self.end_near = half_way if windowed else pieces
            self.mid_near = min(half_way + 1, pieces) if windowed else pieces
            self.end_along = min(self.end_near + 1, pieces) if windowed else pieces

        def along_takes(self, zz, p):
            if not self.windowed:
                return True
            return jnp.logical_not(is_end(zz)) | ((p - 2 * zz + self.pieces) % self.pieces < self.end_along)

        def near_takes(self, cc, p):
            if not self.windowed:
                return True
            reach = jnp.where(is_end(z), self.end_near, self.mid_near)
            return (p - cc + self.pieces) % self.pieces < reach

        def copy(self, origin, kind, target, first, count, group, src=None):
            cols = pl.ds(pl.multiple_of(first * self.width, self.width), count * self.width)
            view = self.buf.at[rows(origin * sh, sh), cols]
            return send(
                view if src is None else src.at[:, cols], view,
                self.sems.at[kind, origin], self.recv.at[origin, group], target,
            )

        def when(self, gate, fn):
            if gate is True:
                fn()
            else:
                pl.when(gate)(fn)

        def along(self, origin, kind, group, src=None):
            to = z + 1 if kind == UP else z - 1
            for i in range(self.size):
                p = group * self.size + i
                self.when(self.along_takes(to, p), lambda: self.copy(
                    origin, kind, index(to, y, c), p, 1, group, src).start())

        def detours(self, plane):
            if self.windowed or depth < 4:
                return False
            return ((z == 1) & (plane == 0)) | ((z == depth - 2) & (plane == depth - 1))

        def near_by(self, origin, group, src=None):
            detour = self.detours(origin // 4)
            for i in range(self.size):
                p = group * self.size + i
                takes = self.near_takes(z * 2 + 1 - y, p)
                if detour is not False:
                    takes = jnp.logical_not(detour)
                self.when(takes, lambda: self.copy(
                    origin, SIDE, side, p, 1, 0, src).start())
                self.when(self.near_takes(chip, p), lambda: self.copy(
                    origin, CORE, peer, p, 1, 0, src).start())

        def each(self, fn):
            if self.groups == 1:
                fn(0)
            else:
                pl.loop(0, self.groups)(fn)

        def own_along(self, src=None, hops=None):
            def go(group):
                @pl.when((z + 1 < depth) & (True if hops is None else z == hops))
                def _():
                    self.along(me, UP, group, src)

                @pl.when((z > 0) & (True if hops is None else depth - 1 - z == hops))
                def _():
                    self.along(me, DOWN, group, src)

            self.each(go)

        def own_near(self, src=None):
            self.each(lambda group: self.near_by(me, group, src))

        def came(self, origin, group):
            def take(count):
                self.copy(origin, CORE, peer, 0, count, group).wait_recv()

            if not self.windowed:
                take(self.size)
                return
            got = sum(
                self.along_takes(z, group * self.size + i).astype(jnp.int32) for i in range(self.size)
            )
            for count in range(1, self.size + 1):
                pl.when(got == count)(functools.partial(take, count))

        def column(self, k, near=True):
            def go(group):
                @pl.when(z - k >= 0)
                def _():
                    origin = index(z - k, y, c)
                    self.came(origin, group)

                    @pl.when(z + 1 < depth)
                    def _():
                        self.along(origin, UP, group)

                    if near:
                        self.near_by(origin, group)

                @pl.when(z + k < depth)
                def _():
                    origin = index(z + k, y, c)
                    self.came(origin, group)

                    @pl.when(z > 0)
                    def _():
                        self.along(origin, DOWN, group)

                    if near:
                        self.near_by(origin, group)

            self.each(go)

        def column_near(self, k):
            def go(group):
                @pl.when(z - k >= 0)
                def _():
                    self.near_by(index(z - k, y, c), group)

                @pl.when(z + k < depth)
                def _():
                    self.near_by(index(z + k, y, c), group)

            self.each(go)

        def by_end(self, fn):
            if self.end_near == self.mid_near:
                fn(self.end_near)
            else:
                pl.when(is_end(z))(functools.partial(fn, self.end_near))
                pl.when(jnp.logical_not(is_end(z)))(functools.partial(fn, self.mid_near))

        def across(self, plane):
            origin = index(plane, 1 - y, c)
            self.by_end(lambda count: self.copy(origin, CORE, peer, 0, count, 0).wait_recv())

            def go(group):
                for i in range(self.size):
                    p = group * self.size + i
                    self.when(self.near_takes(chip, p), lambda: self.copy(
                        origin, CORE, peer, p, 1, 0).start())

            self.each(go)
            if self.detours(plane) is False:
                return

            @pl.when((plane == z) & (z == 0))
            def _():
                self.copy(origin, UP, index(1, y, c), 0, self.pieces, 0).start()

            @pl.when((plane == z) & (z == depth - 1))
            def _():
                self.copy(origin, DOWN, index(depth - 2, y, c), 0, self.pieces, 0).start()

        def whole(self, plane):
            def take(count):
                self.copy(index(plane, 0, 1 - c), CORE, peer, 0, count, 0).wait_recv()
                self.copy(index(plane, 1, 1 - c), CORE, peer, 0, count, 0).wait_recv()

            self.by_end(take)

        def drain(self):
            def sent(origin, kind, count):
                self.copy(origin, kind, peer, 0, count, 0).wait_send()

            for plane in range(depth):
                origin = index(plane, y, c)
                for kind, to, gate in (
                    (UP, z + 1, (plane <= z) & (z + 1 < depth)),
                    (DOWN, z - 1, (plane >= z) & (z > 0)),
                ):
                    if self.end_along == self.pieces:
                        pl.when(gate)(functools.partial(sent, origin, kind, self.pieces))
                    else:
                        pl.when(gate & is_end(to))(functools.partial(sent, origin, kind, self.end_along))
                        pl.when(gate & jnp.logical_not(is_end(to)))(
                            functools.partial(sent, origin, kind, self.pieces))

                def near(count, origin=origin, plane=plane):
                    detour = self.detours(plane)
                    if detour is False:
                        sent(origin, SIDE, count)
                    else:
                        pl.when(jnp.logical_not(detour))(functools.partial(sent, origin, SIDE, count))
                    sent(origin, CORE, count)
                    sent(index(plane, 1 - y, c), CORE, count)

                self.by_end(near)
            if self.detours(z) is False:
                return
            other = index(z, 1 - y, c)
            pl.when(z == 0)(functools.partial(sent, other, UP, self.pieces))
            pl.when(z == depth - 1)(functools.partial(sent, other, DOWN, self.pieces))

    gx = Gather(xall, x_recv, x_send, chips, 4, True)
    gs = Gather(slab_ref, s_recv, s_send, 2, 2, False)
    gx.own_along(x_ref)
    gx.own_near(x_ref)

    flip = z >= (depth + 1) // 2
    zm = jnp.where(flip, depth - 1 - z, z)

    def plane_at(t):
        near = zm - (t + 1) // 2 if t % 2 else zm + t // 2
        p = jnp.where(t <= 2 * zm, near, t)
        return jnp.where(flip, depth - 1 - p, p)

    block = 4 * sh
    tile = min(256, feat)
    far = (z + depth // 2) % depth
    far_weight = jnp.where(is_end(far), 1.0, 0.5).astype(jnp.float32)

    def project(plane):
        xs = rows(plane * block, block)

        def body(reach):
            @pl.loop(0, feat // tile)
            def _(j):
                fs = rows(j * tile, tile)
                value = jnp.zeros((block, tile), jnp.float32)
                for k in range(reach):
                    cs = rows((chip + k) % chips * (2 * feat), 2 * feat)
                    term = lax.dot_general(
                        xall[xs, cs], fv[fs, cs], (((1,), (1,)), ((), ())),
                        preferred_element_type=jnp.float32,
                    )
                    if k == 0:
                        term = term * 0.5
                    elif k == half_way:
                        term = term * far_weight
                    value = value + term
                high = value.astype(jnp.bfloat16)
                proj[xs, fs] = high
                proj_low[xs, fs] = (value - high.astype(jnp.float32)).astype(jnp.bfloat16)

        gx.by_end(body)

    def cols_copy(d, origin, r):
        start, count = SPLIT[r]
        return send(
            gv.at[:, rows(d * width + start * unit, count * unit)],
            cols_ref.at[rows(origin * sh, sh), pl.ds(start * unit, count * unit)],
            c_send.at[r, d], c_recv.at[r, origin], d,
        )

    def send_cols(r, yy):
        @pl.loop(1, depth)
        def _(k):
            for cc in range(2):
                d = index((z + k) % depth, yy, cc)
                cols_copy(d, me, r).start()

    def send_cols_here(r):
        cols_copy(peer, me, r).start()

    def send_cols_across(r):
        for cc in range(2):
            cols_copy(index(z, 1 - y, cc), me, r).start()

    load_x.wait()
    load_g.wait()
    own_slab = pltpu.make_async_copy(
        gv.at[:, pl.ds(0, slab)], slab_ref.at[rows(me * sh, sh), :], local_sem.at[3]
    )
    own_cols = pltpu.make_async_copy(
        gv.at[:, rows(me * width, width)], cols_ref.at[rows(me * sh, sh), :], local_sem.at[4]
    )
    own_slab.start()
    own_cols.start()
    slab_src = gv.at[:, pl.ds(0, slab)]
    end, middle = is_end(z), jnp.logical_not(is_end(z))
    gs.own_along(slab_src, 0)
    pl.when(end)(lambda: gs.own_near(slab_src))
    load_f.wait()
    load_of.start()
    for k in range(1, depth):
        gx.column(k)
        gs.own_along(slab_src, k)
        if k == max(1, depth - 2):
            pl.when(middle)(lambda: gs.own_near(slab_src))
        plane = plane_at(k - 1)
        gx.across(plane)
        gx.whole(plane)
        project(plane)
        if k == 1:
            pl.when(end)(lambda: gs.across(z))

    @pl.when(middle)
    def _():
        gs.column(1)
        send_cols(0, y)

    plane = plane_at(depth - 1)
    gx.across(plane)
    gx.whole(plane)
    project(plane)

    own_features = rows(me * feat, feat)
    size = tokens // BLOCKS
    half = PACKED * size // 2
    share = half // chips

    spot = 0
    for a in range(BLOCKS):
        some, rest = pl.ds(a * size, size), pl.ds(a * size, tokens - a * size)
        total = jnp.zeros((size, tokens - a * size), jnp.float32)
        for piece in (proj, proj_low):
            for lhs, rhs in ((piece[some, :], xall[rest, own_features]), (xall[some, own_features], piece[rest, :])):
                total = total + lax.dot_general(
                    lhs, rhs, (((1,), (1,)), ((), ())), preferred_element_type=jnp.float32
                )
        for j in range(BLOCKS - a):
            part[pl.ds((spot + j) * size, size), :] = total[:, j * size:(j + 1) * size]
        spot += BLOCKS - a

    kept = rows(c * half, half)
    core_sum = send(part.at[rows((1 - c) * half, half), :], in0, r_send.at[0], r_recv.at[0], peer)
    core_sum.start()

    @pl.when(end)
    def _():
        gs.column(1)
        send_cols(0, y)

    core_sum.wait_recv()
    out1[...] = (part[kept, :] + in0[...]).astype(jnp.bfloat16)

    def chip_at(k):
        return (chip + k) % chips

    def device_of(other):
        return index(other // 2, other % 2, c)

    def scatter(k, other, slot):
        return send(
            out1.at[rows(other * share, share), :], in1.at[slot],
            rs_send.at[other], rs_recv.at[slot], device_of(other),
        )

    for k in range(1, chips):
        scatter(k, chip_at(k), chip).start()
    for k in range(2, min(3, depth)):
        gs.column(k)
    for r in range(1, len(SPLIT)):
        send_cols(r, y)
    for r in range(len(SPLIT)):
        send_cols_here(r)
    pl.when(middle)(lambda: gs.across(z))
    total = part[rows(c * half + chip * share, share), :] + in0[rows(chip * share, share), :]
    for k in range(1, chips):
        scatter(k, chip_at(k), chip_at(k)).wait_recv()
        total = total + in1[chip_at(k)].astype(jnp.float32)
    scale = float(n * feat) ** (-0.5)
    mine = rows(c * half + chip * share, share)
    packed[mine, :] = (total * scale).astype(jnp.bfloat16)

    def spread(other, origin):
        view = packed.at[rows(c * half + origin * share, share), :]
        return send(view, view, ag_send.at[other], ag_recv.at[origin], device_of(other))

    for k in range(1, chips):
        spread(chip_at(k), chip).start()
    for k in range(3, depth):
        gs.column(k)
    send_cols(0, 1 - y)
    send_cols_across(0)
    for t in range(1, depth // 2):
        gs.across(plane_at(t))
    for r in range(1, len(SPLIT)):
        send_cols(r, 1 - y)
        send_cols_across(r)
    for k in range(1, chips):
        spread(chip, chip_at(k)).wait_recv()
    view = packed.at[kept, :]
    core_spread = send(view, view, r_send.at[1], r_recv.at[1], peer)
    core_spread.start()
    for t in range(depth // 2, depth):
        gs.across(plane_at(t))
    core_spread.wait_recv()
    spot = 0
    for a in range(BLOCKS):
        for b in range(a, BLOCKS):
            value = packed[pl.ds(spot * size, size), :]
            final[pl.ds(a * size, size), pl.ds(b * size, size)] = value
            if a != b:
                final[pl.ds(b * size, size), pl.ds(a * size, size)] = (
                    value.astype(jnp.float32).T.astype(jnp.bfloat16)
                )
            spot += 1
    for t in range(depth):
        gs.whole(plane_at(t))
    own_slab.wait()
    own_cols.wait()
    load_of.wait()

    strip = min(512, slab)
    for r, (start, count) in enumerate(SPLIT):
        for k in range(1, n):
            cols_copy(me, (me + k) % n, r).wait_recv()
        some = pl.ds(start * unit, count * unit)
        left = lax.dot_general(
            cols_ref[:, some], final[...], (((0,), (0,)), ((), ())),
            preferred_element_type=jnp.float32,
        ).astype(jnp.bfloat16)
        if r == len(SPLIT) - 1:
            left_ref[...] = left
            continue

        @pl.loop(0, slab // strip)
        def _(j):
            cs = rows(j * strip, strip)
            upd_ref[some, cs] = upd_ref[some, cs] + jnp.dot(
                left, slab_ref[:, cs], preferred_element_type=jnp.float32
            ) * (1.0 / tokens)

    gx.drain()
    gs.drain()
    for r in range(len(SPLIT)):
        for k in range(1, n):
            cols_copy((me + k) % n, me, r).wait_send()
    for copy in (core_sum, core_spread):
        copy.wait_send()
    for k in range(1, chips):
        scatter(k, chip_at(k), chip).wait_send()
        spread(chip_at(k), chip).wait_send()


def exchange(n, x, f, g, of):
    sh, din = x.shape
    feat = f.shape[0]
    tokens, chips = n * sh, n // 2
    width, slab = g.shape[1] // n, of.shape[1]
    size = tokens // BLOCKS
    half = PACKED * size // 2
    bf, f32, dma = jnp.bfloat16, jnp.float32, pltpu.SemaphoreType.DMA
    last = SPLIT[-1][1] * (width // UNITS)
    scratch = [
        ((tokens, din), bf), (f.shape, bf), (g.shape, bf), ((tokens, width), bf),
        ((tokens, feat), bf), ((tokens, feat), bf),
        ((2 * half, size), f32), ((half, size), f32), ((half, size), bf),
        ((chips, half // chips, size), bf), ((2 * half, size), bf), ((tokens, tokens), bf),
    ]
    used = sum(functools.reduce(lambda a, b: a * b, s) * jnp.dtype(t).itemsize for s, t in scratch)
    return pl.pallas_call(
        functools.partial(exchange_kernel, n),
        out_shape=(
            pltpu.VMEM(of.shape, of.dtype), pltpu.VMEM((tokens, slab), bf), pltpu.VMEM((last, tokens), bf),
        ),
        in_specs=[pl.BlockSpec(memory_space=pltpu.HBM)] * 4,
        out_specs=(pl.BlockSpec(memory_space=pltpu.VMEM),) * 3,
        scratch_shapes=[pltpu.VMEM(s, t) for s, t in scratch] + [
            dma((6,)), dma((n, 4)), dma((4, n)), dma((n, 2)), dma((4, n)),
            dma((len(SPLIT), n)), dma((len(SPLIT), n)), dma((2,)), dma((2,)),
            dma((chips,)), dma((chips,)), dma((chips,)), dma((chips,)),
        ],
        compiler_params=pltpu.CompilerParams(
            collective_id=0, has_side_effects=True, vmem_limit_bytes=used + 6 * 1024 * 1024
        ),
    )(*(pltpu.with_memory_space_constraint(v, pltpu.HBM) for v in (x, f, g, of)))


def write_kernel(parts, upd, slab_ref, left, dst, buf, sem, strip_sem):
    tokens, slab = slab_ref.shape
    ready = upd.shape[0] - left.shape[0]
    size = ready // parts
    strips, _, strip = buf.shape

    def copy(i):
        some = pl.ds(i * size, size)
        return pltpu.make_async_copy(upd.at[some, :], dst.at[some, :], sem.at[i])

    def strip_copy(j):
        return pltpu.make_async_copy(
            buf.at[j], dst.at[pl.ds(ready, left.shape[0]), pl.ds(j * strip, strip)], strip_sem.at[j]
        )

    for i in range(parts):
        copy(i).start()
    for j in range(strips):
        cs = pl.ds(j * strip, strip)
        buf[j] = upd[pl.ds(ready, left.shape[0]), cs] + jnp.dot(
            left[...], slab_ref[:, cs], preferred_element_type=jnp.float32
        ) * (1.0 / tokens)
        strip_copy(j).start()
    for i in range(parts):
        copy(i).wait()
    for j in range(strips):
        strip_copy(j).wait()


def write(upd, slab_ref, left):
    strip = min(512, upd.shape[1])
    strips, parts = upd.shape[1] // strip, 8
    return pl.pallas_call(
        functools.partial(write_kernel, parts),
        out_shape=jax.ShapeDtypeStruct(upd.shape, upd.dtype),
        in_specs=[pl.BlockSpec(memory_space=pltpu.VMEM)] * 3,
        out_specs=pl.BlockSpec(memory_space=pl.ANY),
        scratch_shapes=[
            pltpu.VMEM((strips, left.shape[0], strip), upd.dtype),
            pltpu.SemaphoreType.DMA((parts,)), pltpu.SemaphoreType.DMA((strips,)),
        ],
        compiler_params=pltpu.CompilerParams(vmem_limit_bytes=12 * 1024 * 1024),
    )(upd, slab_ref, left)


def per_device(n, inputs, input_factor, out_grads, output_factor):
    return write(*exchange(n, inputs, input_factor, out_grads, output_factor))


def solution(mesh):
    spec = P(("groups", "row"), None)
    return jax.shard_map(
        functools.partial(per_device, mesh.shape["row"]),
        mesh=mesh, in_specs=(spec,) * 4, out_specs=spec, check_vma=False,
    )
```

```python
import functools

import jax
import jax.numpy as jnp
from jax import lax
from jax.experimental import pallas as pl
from jax.experimental.pallas import tpu as pltpu
from jax.sharding import PartitionSpec as P

UP, DOWN, SIDE, CORE = range(4)
BLOCKS = 4
PACKED = BLOCKS * (BLOCKS + 1) // 2
SPLIT = ((0, 2), (2, 2))
UNITS = 4


def exchange_kernel(
    n, x_ref, f_ref, g_ref, of_ref, upd_ref, slab_ref, left_ref,
    xall, fv, gv, cols_ref, proj, proj_low, part, in0, out1, in1, packed, final,
    local_sem, x_recv, x_send, s_recv, s_send, c_recv, c_send,
    r_recv, r_send, rs_recv, rs_send, ag_recv, ag_send,
):
    me = lax.axis_index("row")
    depth = n // 4
    z, y, c = me // 4, (me // 2) % 2, me % 2
    sh = x_ref.shape[0]
    tokens = n * sh
    slab = slab_ref.shape[1]
    width = cols_ref.shape[1]
    unit = width // UNITS
    feat = f_ref.shape[0]
    chips = n // 2
    chip = z * 2 + y
    half_way = chips // 2

    def index(zz, yy, cc):
        return zz * 4 + yy * 2 + cc

    side, peer = index(z, 1 - y, c), index(z, y, 1 - c)

    def rows(start, size):
        return pl.ds(pl.multiple_of(start, size), size)

    def is_end(zz):
        return (zz == 0) | (zz == depth - 1)

    load_f = pltpu.make_async_copy(f_ref, fv, local_sem.at[0])
    load_x = pltpu.make_async_copy(x_ref, xall.at[rows(me * sh, sh), :], local_sem.at[1])
    load_g = pltpu.make_async_copy(g_ref, gv, local_sem.at[2])
    load_of = pltpu.make_async_copy(of_ref, upd_ref, local_sem.at[5])
    load_x.start()
    load_g.start()
    load_f.start()

    barrier = pltpu.get_barrier_semaphore()
    for k in range(1, n):
        pl.semaphore_signal(
            barrier, inc=1, device_id={"row": (me + k) % n}, device_id_type=pl.DeviceIdType.MESH
        )
    pl.semaphore_wait(barrier, n - 1)

    def send(src, dst, send_sem, recv_sem, target):
        return pltpu.make_async_remote_copy(
            src_ref=src, dst_ref=dst, send_sem=send_sem, recv_sem=recv_sem,
            device_id={"row": target}, device_id_type=pl.DeviceIdType.MESH,
        )

    class Gather:
        def __init__(self, buf, recv, sems, pieces, groups, windowed):
            self.buf, self.recv, self.sems = buf, recv, sems
            self.pieces, self.groups, self.windowed = pieces, groups, windowed
            self.width = buf.shape[1] // pieces
            self.size = pieces // groups
            self.end_near = half_way if windowed else pieces
            self.mid_near = min(half_way + 1, pieces) if windowed else pieces
            self.end_along = min(self.end_near + 1, pieces) if windowed else pieces

        def along_takes(self, zz, p):
            if not self.windowed:
                return True
            return jnp.logical_not(is_end(zz)) | ((p - 2 * zz + self.pieces) % self.pieces < self.end_along)

        def near_takes(self, cc, p):
            if not self.windowed:
                return True
            reach = jnp.where(is_end(z), self.end_near, self.mid_near)
            return (p - cc + self.pieces) % self.pieces < reach

        def copy(self, origin, kind, target, first, count, group, src=None):
            cols = pl.ds(pl.multiple_of(first * self.width, self.width), count * self.width)
            view = self.buf.at[rows(origin * sh, sh), cols]
            return send(
                view if src is None else src.at[:, cols], view,
                self.sems.at[kind, origin], self.recv.at[origin, group], target,
            )

        def when(self, gate, fn):
            if gate is True:
                fn()
            else:
                pl.when(gate)(fn)

        def along(self, origin, kind, group, src=None):
            to = z + 1 if kind == UP else z - 1
            for i in range(self.size):
                p = group * self.size + i
                self.when(self.along_takes(to, p), lambda: self.copy(
                    origin, kind, index(to, y, c), p, 1, group, src).start())

        def detours(self, plane):
            if self.windowed or depth < 4:
                return False
            return ((z == 1) & (plane == 0)) | ((z == depth - 2) & (plane == depth - 1))

        def near_by(self, origin, group, src=None):
            detour = self.detours(origin // 4)
            for i in range(self.size):
                p = group * self.size + i
                takes = self.near_takes(z * 2 + 1 - y, p)
                if detour is not False:
                    takes = jnp.logical_not(detour)
                self.when(takes, lambda: self.copy(
                    origin, SIDE, side, p, 1, 0, src).start())
                self.when(self.near_takes(chip, p), lambda: self.copy(
                    origin, CORE, peer, p, 1, 0, src).start())

        def each(self, fn):
            if self.groups == 1:
                fn(0)
            else:
                pl.loop(0, self.groups)(fn)

        def own_along(self, src=None, hops=None):
            def go(group):
                @pl.when((z + 1 < depth) & (True if hops is None else z == hops))
                def _():
                    self.along(me, UP, group, src)

                @pl.when((z > 0) & (True if hops is None else depth - 1 - z == hops))
                def _():
                    self.along(me, DOWN, group, src)

            self.each(go)

        def own_near(self, src=None):
            self.each(lambda group: self.near_by(me, group, src))

        def came(self, origin, group):
            def take(count):
                self.copy(origin, CORE, peer, 0, count, group).wait_recv()

            if not self.windowed:
                take(self.size)
                return
            got = sum(
                self.along_takes(z, group * self.size + i).astype(jnp.int32) for i in range(self.size)
            )
            for count in range(1, self.size + 1):
                pl.when(got == count)(functools.partial(take, count))

        def column(self, k, near=True):
            def go(group):
                @pl.when(z - k >= 0)
                def _():
                    origin = index(z - k, y, c)
                    self.came(origin, group)

                    @pl.when(z + 1 < depth)
                    def _():
                        self.along(origin, UP, group)

                    if near:
                        self.near_by(origin, group)

                @pl.when(z + k < depth)
                def _():
                    origin = index(z + k, y, c)
                    self.came(origin, group)

                    @pl.when(z > 0)
                    def _():
                        self.along(origin, DOWN, group)

                    if near:
                        self.near_by(origin, group)

            self.each(go)

        def column_near(self, k):
            def go(group):
                @pl.when(z - k >= 0)
                def _():
                    self.near_by(index(z - k, y, c), group)

                @pl.when(z + k < depth)
                def _():
                    self.near_by(index(z + k, y, c), group)

            self.each(go)

        def by_end(self, fn):
            if self.end_near == self.mid_near:
                fn(self.end_near)
            else:
                pl.when(is_end(z))(functools.partial(fn, self.end_near))
                pl.when(jnp.logical_not(is_end(z)))(functools.partial(fn, self.mid_near))

        def across(self, plane):
            origin = index(plane, 1 - y, c)
            self.by_end(lambda count: self.copy(origin, CORE, peer, 0, count, 0).wait_recv())

            def go(group):
                for i in range(self.size):
                    p = group * self.size + i
                    self.when(self.near_takes(chip, p), lambda: self.copy(
                        origin, CORE, peer, p, 1, 0).start())

            self.each(go)
            if self.detours(plane) is False:
                return

            @pl.when((plane == z) & (z == 0))
            def _():
                self.copy(origin, UP, index(1, y, c), 0, self.pieces, 0).start()

            @pl.when((plane == z) & (z == depth - 1))
            def _():
                self.copy(origin, DOWN, index(depth - 2, y, c), 0, self.pieces, 0).start()

        def whole(self, plane):
            def take(count):
                self.copy(index(plane, 0, 1 - c), CORE, peer, 0, count, 0).wait_recv()
                self.copy(index(plane, 1, 1 - c), CORE, peer, 0, count, 0).wait_recv()

            self.by_end(take)

        def drain(self):
            def sent(origin, kind, count):
                self.copy(origin, kind, peer, 0, count, 0).wait_send()

            for plane in range(depth):
                origin = index(plane, y, c)
                for kind, to, gate in (
                    (UP, z + 1, (plane <= z) & (z + 1 < depth)),
                    (DOWN, z - 1, (plane >= z) & (z > 0)),
                ):
                    if self.end_along == self.pieces:
                        pl.when(gate)(functools.partial(sent, origin, kind, self.pieces))
                    else:
                        pl.when(gate & is_end(to))(functools.partial(sent, origin, kind, self.end_along))
                        pl.when(gate & jnp.logical_not(is_end(to)))(
                            functools.partial(sent, origin, kind, self.pieces))

                def near(count, origin=origin, plane=plane):
                    detour = self.detours(plane)
                    if detour is False:
                        sent(origin, SIDE, count)
                    else:
                        pl.when(jnp.logical_not(detour))(functools.partial(sent, origin, SIDE, count))
                    sent(origin, CORE, count)
                    sent(index(plane, 1 - y, c), CORE, count)

                self.by_end(near)
            if self.detours(z) is False:
                return
            other = index(z, 1 - y, c)
            pl.when(z == 0)(functools.partial(sent, other, UP, self.pieces))
            pl.when(z == depth - 1)(functools.partial(sent, other, DOWN, self.pieces))

    gx = Gather(xall, x_recv, x_send, chips, 4, True)
    gs = Gather(slab_ref, s_recv, s_send, 2, 2, False)
    gx.own_along(x_ref)
    gx.own_near(x_ref)

    flip = z >= (depth + 1) // 2
    zm = jnp.where(flip, depth - 1 - z, z)

    def plane_at(t):
        near = zm - (t + 1) // 2 if t % 2 else zm + t // 2
        p = jnp.where(t <= 2 * zm, near, t)
        return jnp.where(flip, depth - 1 - p, p)

    block = 4 * sh
    tile = min(256, feat)
    far = (z + depth // 2) % depth
    far_weight = jnp.where(is_end(far), 1.0, 0.5).astype(jnp.float32)

    def project(plane):
        xs = rows(plane * block, block)

        def body(reach):
            @pl.loop(0, feat // tile)
            def _(j):
                fs = rows(j * tile, tile)
                value = jnp.zeros((block, tile), jnp.float32)
                for k in range(reach):
                    cs = rows((chip + k) % chips * (2 * feat), 2 * feat)
                    term = lax.dot_general(
                        xall[xs, cs], fv[fs, cs], (((1,), (1,)), ((), ())),
                        preferred_element_type=jnp.float32,
                    )
                    if k == 0:
                        term = term * 0.5
                    elif k == half_way:
                        term = term * far_weight
                    value = value + term
                high = value.astype(jnp.bfloat16)
                proj[xs, fs] = high
                proj_low[xs, fs] = (value - high.astype(jnp.float32)).astype(jnp.bfloat16)

        gx.by_end(body)

    def cols_copy(d, origin, r):
        start, count = SPLIT[r]
        return send(
            gv.at[:, rows(d * width + start * unit, count * unit)],
            cols_ref.at[rows(origin * sh, sh), pl.ds(start * unit, count * unit)],
            c_send.at[r, d], c_recv.at[r, origin], d,
        )

    every = range(len(SPLIT))
    beside = (z == 1) | (z == depth - 2)
    close = jnp.where(z == 1, 0, depth - 1)

    def send_cols_to(r, zz, yy):
        for cc in range(2):
            cols_copy(index(zz, yy, cc), me, r).start()

    def send_cols_along(r, ends):
        @pl.loop(1, depth)
        def _(k):
            zz = (z + k) % depth

            @pl.when((is_end(zz) == ends) & jnp.logical_not(beside & (zz == close)))
            def _():
                send_cols_to(r, zz, y)

    def send_cols_close():
        @pl.when(beside)
        def _():
            for r in every:
                send_cols_to(r, close, y)

    def send_cols_side(r):
        send_cols_to(r, z, 1 - y)

    def send_cols_across(r, ends):
        if not ends:
            pl.when(jnp.logical_not(is_end(z)))(lambda: send_cols_side(r))

        @pl.loop(1, depth)
        def _(k):
            zz = (z + k) % depth
            pl.when(is_end(zz) == ends)(lambda: send_cols_to(r, zz, 1 - y))

    load_x.wait()
    load_g.wait()
    own_slab = pltpu.make_async_copy(
        gv.at[:, pl.ds(0, slab)], slab_ref.at[rows(me * sh, sh), :], local_sem.at[3]
    )
    own_cols = pltpu.make_async_copy(
        gv.at[:, rows(me * width, width)], cols_ref.at[rows(me * sh, sh), :], local_sem.at[4]
    )
    own_slab.start()
    own_cols.start()
    slab_src = gv.at[:, pl.ds(0, slab)]
    end, middle = is_end(z), jnp.logical_not(is_end(z))
    gs.own_along(slab_src, 0)

    @pl.when(end)
    def _():
        gs.own_near(slab_src)
        for r in every:
            send_cols_side(r)

    load_f.wait()
    load_of.start()
    for k in range(1, depth):
        gx.column(k)
        gs.own_along(slab_src, k)
        if k == 1:
            send_cols_close()
        if k == max(1, depth - 2):
            pl.when(middle)(lambda: gs.own_near(slab_src))
        plane = plane_at(k - 1)
        gx.across(plane)
        gx.whole(plane)
        project(plane)
        if k == 1:
            pl.when(end)(lambda: gs.across(z))

    gs.column(1)
    plane = plane_at(depth - 1)
    gx.across(plane)
    gx.whole(plane)
    project(plane)

    own_features = rows(me * feat, feat)
    size = tokens // BLOCKS
    share = PACKED * size // chips

    spot = 0
    for a in range(BLOCKS):
        some, rest = pl.ds(a * size, size), pl.ds(a * size, tokens - a * size)
        total = jnp.zeros((size, tokens - a * size), jnp.float32)
        for piece in (proj, proj_low):
            for lhs, rhs in ((piece[some, :], xall[rest, own_features]), (xall[some, own_features], piece[rest, :])):
                total = total + lax.dot_general(
                    lhs, rhs, (((1,), (1,)), ((), ())), preferred_element_type=jnp.float32
                )
        for j in range(BLOCKS - a):
            part[pl.ds((spot + j) * size, size), :] = total[:, j * size:(j + 1) * size]
        spot += BLOCKS - a

    sums, bulk = c == 1, c == 0
    core_sum = send(part, in0, r_send.at[0], r_recv.at[0], peer)
    pl.when(bulk)(lambda: core_sum.start())

    def chip_at(k):
        return (chip + k) % chips

    def device_of(other):
        return index(other // 2, other % 2, c)

    def scatter(k, other, slot):
        return send(
            out1.at[rows(other * share, share), :], in1.at[slot],
            rs_send.at[other], rs_recv.at[slot], device_of(other),
        )

    def spread(other, origin):
        view = packed.at[rows(origin * share, share), :]
        return send(view, view, ag_send.at[other], ag_recv.at[origin], device_of(other))

    @pl.when(sums)
    def _():
        core_sum.wait_recv()
        out1[...] = (part[...] + in0[...]).astype(jnp.bfloat16)
        for k in range(1, chips):
            scatter(k, chip_at(k), chip).start()

    @pl.when(bulk)
    def _():
        for r in every:
            send_cols_along(r, False)

    for k in range(2, min(3, depth)):
        gs.column(k)

    @pl.when(sums)
    def _():
        mine = rows(chip * share, share)
        total = part[mine, :] + in0[mine, :]
        for k in range(1, chips):
            scatter(k, chip_at(k), chip_at(k)).wait_recv()
            total = total + in1[chip_at(k)].astype(jnp.float32)
        packed[mine, :] = (total * float(n * feat) ** (-0.5)).astype(jnp.bfloat16)
        for k in range(1, chips):
            spread(chip_at(k), chip).start()
        for r in every:
            send_cols_along(r, False)

    for k in range(3, depth):
        gs.column(k)
    for r in every:
        send_cols_across(r, False)
    send_cols_along(0, True)
    pl.when(middle)(lambda: gs.across(z))
    for r in every:
        cols_copy(peer, me, r).start()
    send_cols_across(0, True)
    for r in every[1:]:
        send_cols_along(r, True)
        send_cols_across(r, True)
    for t in range(1, depth // 2):
        gs.across(plane_at(t))
    core_spread = send(packed, packed, r_send.at[1], r_recv.at[1], peer)

    @pl.when(sums)
    def _():
        for k in range(1, chips):
            spread(chip, chip_at(k)).wait_recv()
        core_spread.start()

    for t in range(depth // 2, depth):
        gs.across(plane_at(t))
    pl.when(bulk)(lambda: core_spread.wait_recv())
    spot = 0
    for a in range(BLOCKS):
        for b in range(a, BLOCKS):
            value = packed[pl.ds(spot * size, size), :]
            final[pl.ds(a * size, size), pl.ds(b * size, size)] = value
            if a != b:
                final[pl.ds(b * size, size), pl.ds(a * size, size)] = (
                    value.astype(jnp.float32).T.astype(jnp.bfloat16)
                )
            spot += 1
    for t in range(depth):
        gs.whole(plane_at(t))
    own_slab.wait()
    own_cols.wait()
    load_of.wait()

    strip = min(512, slab)
    for r, (start, count) in enumerate(SPLIT):
        for k in range(1, n):
            cols_copy(me, (me + k) % n, r).wait_recv()
        some = pl.ds(start * unit, count * unit)
        left = lax.dot_general(
            cols_ref[:, some], final[...], (((0,), (0,)), ((), ())),
            preferred_element_type=jnp.float32,
        ).astype(jnp.bfloat16)
        if r == len(SPLIT) - 1:
            left_ref[...] = left
            continue

        @pl.loop(0, slab // strip)
        def _(j):
            cs = rows(j * strip, strip)
            upd_ref[some, cs] = upd_ref[some, cs] + jnp.dot(
                left, slab_ref[:, cs], preferred_element_type=jnp.float32
            ) * (1.0 / tokens)

    gx.drain()
    gs.drain()
    for r in range(len(SPLIT)):
        for k in range(1, n):
            cols_copy((me + k) % n, me, r).wait_send()
    pl.when(bulk)(lambda: core_sum.wait_send())

    @pl.when(sums)
    def _():
        core_spread.wait_send()
        for k in range(1, chips):
            scatter(k, chip_at(k), chip).wait_send()
            spread(chip_at(k), chip).wait_send()


def exchange(n, x, f, g, of):
    sh, din = x.shape
    feat = f.shape[0]
    tokens, chips = n * sh, n // 2
    width, slab = g.shape[1] // n, of.shape[1]
    size = tokens // BLOCKS
    packed = PACKED * size
    bf, f32, dma = jnp.bfloat16, jnp.float32, pltpu.SemaphoreType.DMA
    last = SPLIT[-1][1] * (width // UNITS)
    scratch = [
        ((tokens, din), bf), (f.shape, bf), (g.shape, bf), ((tokens, width), bf),
        ((tokens, feat), bf), ((tokens, feat), bf),
        ((packed, size), f32), ((packed, size), f32), ((packed, size), bf),
        ((chips, packed // chips, size), bf), ((packed, size), bf), ((tokens, tokens), bf),
    ]
    used = sum(functools.reduce(lambda a, b: a * b, s) * jnp.dtype(t).itemsize for s, t in scratch)
    return pl.pallas_call(
        functools.partial(exchange_kernel, n),
        out_shape=(
            pltpu.VMEM(of.shape, of.dtype), pltpu.VMEM((tokens, slab), bf), pltpu.VMEM((last, tokens), bf),
        ),
        in_specs=[pl.BlockSpec(memory_space=pltpu.HBM)] * 4,
        out_specs=(pl.BlockSpec(memory_space=pltpu.VMEM),) * 3,
        scratch_shapes=[pltpu.VMEM(s, t) for s, t in scratch] + [
            dma((6,)), dma((n, 4)), dma((4, n)), dma((n, 2)), dma((4, n)),
            dma((len(SPLIT), n)), dma((len(SPLIT), n)), dma((2,)), dma((2,)),
            dma((chips,)), dma((chips,)), dma((chips,)), dma((chips,)),
        ],
        compiler_params=pltpu.CompilerParams(
            collective_id=0, has_side_effects=True, vmem_limit_bytes=used + 3 * 1024 * 1024
        ),
    )(*(pltpu.with_memory_space_constraint(v, pltpu.HBM) for v in (x, f, g, of)))


def write_kernel(parts, upd, slab_ref, left, dst, buf, sem, strip_sem):
    tokens, slab = slab_ref.shape
    ready = upd.shape[0] - left.shape[0]
    size = ready // parts
    strips, _, strip = buf.shape

    def copy(i):
        some = pl.ds(i * size, size)
        return pltpu.make_async_copy(upd.at[some, :], dst.at[some, :], sem.at[i])

    def strip_copy(j):
        return pltpu.make_async_copy(
            buf.at[j], dst.at[pl.ds(ready, left.shape[0]), pl.ds(j * strip, strip)], strip_sem.at[j]
        )

    for i in range(parts):
        copy(i).start()
    for j in range(strips):
        cs = pl.ds(j * strip, strip)
        buf[j] = upd[pl.ds(ready, left.shape[0]), cs] + jnp.dot(
            left[...], slab_ref[:, cs], preferred_element_type=jnp.float32
        ) * (1.0 / tokens)
        strip_copy(j).start()
    for i in range(parts):
        copy(i).wait()
    for j in range(strips):
        strip_copy(j).wait()


def write(upd, slab_ref, left):
    strip = min(512, upd.shape[1])
    strips, parts = upd.shape[1] // strip, 8
    return pl.pallas_call(
        functools.partial(write_kernel, parts),
        out_shape=jax.ShapeDtypeStruct(upd.shape, upd.dtype),
        in_specs=[pl.BlockSpec(memory_space=pltpu.VMEM)] * 3,
        out_specs=pl.BlockSpec(memory_space=pl.ANY),
        scratch_shapes=[
            pltpu.VMEM((strips, left.shape[0], strip), upd.dtype),
            pltpu.SemaphoreType.DMA((parts,)), pltpu.SemaphoreType.DMA((strips,)),
        ],
        compiler_params=pltpu.CompilerParams(vmem_limit_bytes=12 * 1024 * 1024),
    )(upd, slab_ref, left)


def per_device(n, inputs, input_factor, out_grads, output_factor):
    return write(*exchange(n, inputs, input_factor, out_grads, output_factor))


def solution(mesh):
    spec = P(("groups", "row"), None)
    return jax.shard_map(
        functools.partial(per_device, mesh.shape["row"]),
        mesh=mesh, in_specs=(spec,) * 4, out_specs=spec, check_vma=False,
    )
```

```python
import functools

import jax
import jax.numpy as jnp
from jax import lax
from jax.experimental import pallas as pl
from jax.experimental.pallas import tpu as pltpu
from jax.sharding import PartitionSpec as P

UP, DOWN, SIDE, CORE = range(4)
BLOCKS = 4
PACKED = BLOCKS * (BLOCKS + 1) // 2
SPLIT = ((0, 1), (1, 3))
UNITS = 4


def exchange_kernel(
    n, x_ref, f_ref, g_ref, of_ref, upd_ref, slab_ref, left_ref,
    xall, fv, gv, cols_ref, proj, proj_low, part, in0, out1, in1, packed, final,
    local_sem, x_recv, x_send, s_recv, s_send, c_recv, c_send,
    r_recv, r_send, rs_recv, rs_send, ag_recv, ag_send,
):
    me = lax.axis_index("row")
    depth = n // 4
    z, y, c = me // 4, (me // 2) % 2, me % 2
    sh = x_ref.shape[0]
    tokens = n * sh
    slab = slab_ref.shape[1]
    width = cols_ref.shape[1]
    unit = width // UNITS
    feat = f_ref.shape[0]
    chips = n // 2
    chip = z * 2 + y
    half_way = chips // 2

    def index(zz, yy, cc):
        return zz * 4 + yy * 2 + cc

    side, peer = index(z, 1 - y, c), index(z, y, 1 - c)

    def rows(start, size):
        return pl.ds(pl.multiple_of(start, size), size)

    def is_end(zz):
        return (zz == 0) | (zz == depth - 1)

    load_f = pltpu.make_async_copy(f_ref, fv, local_sem.at[0])
    load_x = pltpu.make_async_copy(x_ref, xall.at[rows(me * sh, sh), :], local_sem.at[1])
    load_g = pltpu.make_async_copy(g_ref, gv, local_sem.at[2])
    load_of = pltpu.make_async_copy(of_ref, upd_ref, local_sem.at[5])
    load_x.start()
    load_g.start()
    load_f.start()

    barrier = pltpu.get_barrier_semaphore()
    for k in range(1, n):
        pl.semaphore_signal(
            barrier, inc=1, device_id={"row": (me + k) % n}, device_id_type=pl.DeviceIdType.MESH
        )
    pl.semaphore_wait(barrier, n - 1)

    def send(src, dst, send_sem, recv_sem, target):
        return pltpu.make_async_remote_copy(
            src_ref=src, dst_ref=dst, send_sem=send_sem, recv_sem=recv_sem,
            device_id={"row": target}, device_id_type=pl.DeviceIdType.MESH,
        )

    class Gather:
        def __init__(self, buf, recv, sems, pieces, groups, windowed):
            self.buf, self.recv, self.sems = buf, recv, sems
            self.pieces, self.groups, self.windowed = pieces, groups, windowed
            self.width = buf.shape[1] // pieces
            self.size = pieces // groups
            self.end_near = half_way if windowed else pieces
            self.mid_near = min(half_way + 1, pieces) if windowed else pieces
            self.end_along = min(self.end_near + 1, pieces) if windowed else pieces

        def along_takes(self, zz, p):
            if not self.windowed:
                return True
            return jnp.logical_not(is_end(zz)) | ((p - 2 * zz + self.pieces) % self.pieces < self.end_along)

        def near_takes(self, cc, p):
            if not self.windowed:
                return True
            reach = jnp.where(is_end(z), self.end_near, self.mid_near)
            return (p - cc + self.pieces) % self.pieces < reach

        def copy(self, origin, kind, target, first, count, group, src=None):
            cols = pl.ds(pl.multiple_of(first * self.width, self.width), count * self.width)
            view = self.buf.at[rows(origin * sh, sh), cols]
            return send(
                view if src is None else src.at[:, cols], view,
                self.sems.at[kind, origin], self.recv.at[origin, group], target,
            )

        def when(self, gate, fn):
            if gate is True:
                fn()
            else:
                pl.when(gate)(fn)

        def along(self, origin, kind, group, src=None):
            to = z + 1 if kind == UP else z - 1
            for i in range(self.size):
                p = group * self.size + i
                self.when(self.along_takes(to, p), lambda: self.copy(
                    origin, kind, index(to, y, c), p, 1, group, src).start())

        def detours(self, plane):
            if self.windowed or depth < 4:
                return False
            return ((z == 1) & (plane == 0)) | ((z == depth - 2) & (plane == depth - 1))

        def near_by(self, origin, group, src=None):
            detour = self.detours(origin // 4)
            for i in range(self.size):
                p = group * self.size + i
                takes = self.near_takes(z * 2 + 1 - y, p)
                if detour is not False:
                    takes = jnp.logical_not(detour)
                self.when(takes, lambda: self.copy(
                    origin, SIDE, side, p, 1, 0, src).start())
                self.when(self.near_takes(chip, p), lambda: self.copy(
                    origin, CORE, peer, p, 1, 0, src).start())

        def each(self, fn):
            if self.groups == 1:
                fn(0)
            else:
                pl.loop(0, self.groups)(fn)

        def own_along(self, src=None, hops=None):
            def go(group):
                @pl.when((z + 1 < depth) & (True if hops is None else z == hops))
                def _():
                    self.along(me, UP, group, src)

                @pl.when((z > 0) & (True if hops is None else depth - 1 - z == hops))
                def _():
                    self.along(me, DOWN, group, src)

            self.each(go)

        def own_near(self, src=None):
            self.each(lambda group: self.near_by(me, group, src))

        def came(self, origin, group):
            def take(count):
                self.copy(origin, CORE, peer, 0, count, group).wait_recv()

            if not self.windowed:
                take(self.size)
                return
            got = sum(
                self.along_takes(z, group * self.size + i).astype(jnp.int32) for i in range(self.size)
            )
            for count in range(1, self.size + 1):
                pl.when(got == count)(functools.partial(take, count))

        def column(self, k, near=True):
            def go(group):
                @pl.when(z - k >= 0)
                def _():
                    origin = index(z - k, y, c)
                    self.came(origin, group)

                    @pl.when(z + 1 < depth)
                    def _():
                        self.along(origin, UP, group)

                    if near:
                        self.near_by(origin, group)

                @pl.when(z + k < depth)
                def _():
                    origin = index(z + k, y, c)
                    self.came(origin, group)

                    @pl.when(z > 0)
                    def _():
                        self.along(origin, DOWN, group)

                    if near:
                        self.near_by(origin, group)

            self.each(go)

        def column_near(self, k):
            def go(group):
                @pl.when(z - k >= 0)
                def _():
                    self.near_by(index(z - k, y, c), group)

                @pl.when(z + k < depth)
                def _():
                    self.near_by(index(z + k, y, c), group)

            self.each(go)

        def by_end(self, fn):
            if self.end_near == self.mid_near:
                fn(self.end_near)
            else:
                pl.when(is_end(z))(functools.partial(fn, self.end_near))
                pl.when(jnp.logical_not(is_end(z)))(functools.partial(fn, self.mid_near))

        def across(self, plane):
            origin = index(plane, 1 - y, c)
            self.by_end(lambda count: self.copy(origin, CORE, peer, 0, count, 0).wait_recv())

            def go(group):
                for i in range(self.size):
                    p = group * self.size + i
                    self.when(self.near_takes(chip, p), lambda: self.copy(
                        origin, CORE, peer, p, 1, 0).start())

            self.each(go)
            if self.detours(plane) is False:
                return

            @pl.when((plane == z) & (z == 0))
            def _():
                self.copy(origin, UP, index(1, y, c), 0, self.pieces, 0).start()

            @pl.when((plane == z) & (z == depth - 1))
            def _():
                self.copy(origin, DOWN, index(depth - 2, y, c), 0, self.pieces, 0).start()

        def whole(self, plane):
            def take(count):
                self.copy(index(plane, 0, 1 - c), CORE, peer, 0, count, 0).wait_recv()
                self.copy(index(plane, 1, 1 - c), CORE, peer, 0, count, 0).wait_recv()

            self.by_end(take)

        def drain(self):
            def sent(origin, kind, count):
                self.copy(origin, kind, peer, 0, count, 0).wait_send()

            for plane in range(depth):
                origin = index(plane, y, c)
                for kind, to, gate in (
                    (UP, z + 1, (plane <= z) & (z + 1 < depth)),
                    (DOWN, z - 1, (plane >= z) & (z > 0)),
                ):
                    if self.end_along == self.pieces:
                        pl.when(gate)(functools.partial(sent, origin, kind, self.pieces))
                    else:
                        pl.when(gate & is_end(to))(functools.partial(sent, origin, kind, self.end_along))
                        pl.when(gate & jnp.logical_not(is_end(to)))(
                            functools.partial(sent, origin, kind, self.pieces))

                def near(count, origin=origin, plane=plane):
                    detour = self.detours(plane)
                    if detour is False:
                        sent(origin, SIDE, count)
                    else:
                        pl.when(jnp.logical_not(detour))(functools.partial(sent, origin, SIDE, count))
                    sent(origin, CORE, count)
                    sent(index(plane, 1 - y, c), CORE, count)

                self.by_end(near)
            if self.detours(z) is False:
                return
            other = index(z, 1 - y, c)
            pl.when(z == 0)(functools.partial(sent, other, UP, self.pieces))
            pl.when(z == depth - 1)(functools.partial(sent, other, DOWN, self.pieces))

    gx = Gather(xall, x_recv, x_send, chips, 4, True)
    gs = Gather(slab_ref, s_recv, s_send, 2, 2, False)
    gx.own_along(x_ref)
    gx.own_near(x_ref)

    flip = z >= (depth + 1) // 2
    zm = jnp.where(flip, depth - 1 - z, z)

    def plane_at(t):
        near = zm - (t + 1) // 2 if t % 2 else zm + t // 2
        p = jnp.where(t <= 2 * zm, near, t)
        return jnp.where(flip, depth - 1 - p, p)

    block = 4 * sh
    tile = min(256, feat)
    far = (z + depth // 2) % depth
    far_weight = jnp.where(is_end(far), 1.0, 0.5).astype(jnp.float32)

    def project(plane):
        xs = rows(plane * block, block)

        def body(reach):
            @pl.loop(0, feat // tile)
            def _(j):
                fs = rows(j * tile, tile)
                value = jnp.zeros((block, tile), jnp.float32)
                for k in range(reach):
                    cs = rows((chip + k) % chips * (2 * feat), 2 * feat)
                    term = lax.dot_general(
                        xall[xs, cs], fv[fs, cs], (((1,), (1,)), ((), ())),
                        preferred_element_type=jnp.float32,
                    )
                    if k == 0:
                        term = term * 0.5
                    elif k == half_way:
                        term = term * far_weight
                    value = value + term
                high = value.astype(jnp.bfloat16)
                proj[xs, fs] = high
                proj_low[xs, fs] = (value - high.astype(jnp.float32)).astype(jnp.bfloat16)

        gx.by_end(body)

    def cols_copy(d, origin, r):
        start, count = SPLIT[r]
        return send(
            gv.at[:, pl.ds(pl.multiple_of(d * width + start * unit, unit), count * unit)],
            cols_ref.at[rows(origin * sh, sh), pl.ds(start * unit, count * unit)],
            c_send.at[r, d], c_recv.at[r, origin], d,
        )

    every = range(len(SPLIT))
    beside = (z == 1) | (z == depth - 2)
    close = jnp.where(z == 1, 0, depth - 1)

    def send_cols_to(r, zz, yy):
        for cc in range(2):
            cols_copy(index(zz, yy, cc), me, r).start()

    def send_cols_along(r, ends):
        @pl.loop(1, depth)
        def _(k):
            zz = (z + k) % depth

            @pl.when((is_end(zz) == ends) & jnp.logical_not(beside & (zz == close)))
            def _():
                send_cols_to(r, zz, y)

    def send_cols_close():
        @pl.when(beside)
        def _():
            for r in every:
                send_cols_to(r, close, y)

    def send_cols_side(r):
        send_cols_to(r, z, 1 - y)

    def send_cols_across(r, ends):
        if not ends:
            pl.when(jnp.logical_not(is_end(z)))(lambda: send_cols_side(r))

        @pl.loop(1, depth)
        def _(k):
            zz = (z + k) % depth
            pl.when(is_end(zz) == ends)(lambda: send_cols_to(r, zz, 1 - y))

    load_x.wait()
    load_g.wait()
    own_slab = pltpu.make_async_copy(
        gv.at[:, pl.ds(0, slab)], slab_ref.at[rows(me * sh, sh), :], local_sem.at[3]
    )
    own_cols = pltpu.make_async_copy(
        gv.at[:, rows(me * width, width)], cols_ref.at[rows(me * sh, sh), :], local_sem.at[4]
    )
    own_slab.start()
    own_cols.start()
    slab_src = gv.at[:, pl.ds(0, slab)]
    end, middle = is_end(z), jnp.logical_not(is_end(z))
    gs.own_along(slab_src, 0)

    @pl.when(end)
    def _():
        gs.own_near(slab_src)
        for r in every:
            send_cols_side(r)

    load_f.wait()
    load_of.start()
    for k in range(1, depth):
        gx.column(k)
        gs.own_along(slab_src, k)
        if k == 1:
            send_cols_close()
        if k == max(1, depth - 2):
            pl.when(middle)(lambda: gs.own_near(slab_src))
        plane = plane_at(k - 1)
        gx.across(plane)
        gx.whole(plane)
        project(plane)
        if k == 1:
            pl.when(end)(lambda: gs.across(z))

    gs.column(1)
    plane = plane_at(depth - 1)
    gx.across(plane)
    gx.whole(plane)
    project(plane)

    own_features = rows(me * feat, feat)
    size = tokens // BLOCKS
    share = PACKED * size // chips

    spot = 0
    for a in range(BLOCKS):
        some, rest = pl.ds(a * size, size), pl.ds(a * size, tokens - a * size)
        total = jnp.zeros((size, tokens - a * size), jnp.float32)
        for piece in (proj, proj_low):
            for lhs, rhs in ((piece[some, :], xall[rest, own_features]), (xall[some, own_features], piece[rest, :])):
                total = total + lax.dot_general(
                    lhs, rhs, (((1,), (1,)), ((), ())), preferred_element_type=jnp.float32
                )
        for j in range(BLOCKS - a):
            part[pl.ds((spot + j) * size, size), :] = total[:, j * size:(j + 1) * size]
        spot += BLOCKS - a

    sums, bulk = c == 1, c == 0
    core_sum = send(part, in0, r_send.at[0], r_recv.at[0], peer)
    pl.when(bulk)(lambda: core_sum.start())

    def chip_at(k):
        return (chip + k) % chips

    def device_of(other):
        return index(other // 2, other % 2, c)

    def scatter(k, other, slot):
        return send(
            out1.at[rows(other * share, share), :], in1.at[slot],
            rs_send.at[other], rs_recv.at[slot], device_of(other),
        )

    def spread(other, origin):
        view = packed.at[rows(origin * share, share), :]
        return send(view, view, ag_send.at[other], ag_recv.at[origin], device_of(other))

    @pl.when(sums)
    def _():
        core_sum.wait_recv()
        out1[...] = (part[...] + in0[...]).astype(jnp.bfloat16)
        for k in range(1, chips):
            scatter(k, chip_at(k), chip).start()

    @pl.when(bulk)
    def _():
        for r in every:
            send_cols_along(r, False)

    for k in range(2, min(3, depth)):
        gs.column(k)

    @pl.when(sums)
    def _():
        mine = rows(chip * share, share)
        total = part[mine, :] + in0[mine, :]
        for k in range(1, chips):
            scatter(k, chip_at(k), chip_at(k)).wait_recv()
            total = total + in1[chip_at(k)].astype(jnp.float32)
        packed[mine, :] = (total * float(n * feat) ** (-0.5)).astype(jnp.bfloat16)
        for k in range(1, chips):
            spread(chip_at(k), chip).start()
        for r in every:
            send_cols_along(r, False)

    for k in range(3, depth):
        gs.column(k)
    for r in every:
        send_cols_across(r, False)
    send_cols_along(0, True)
    pl.when(middle)(lambda: gs.across(z))
    for r in every:
        cols_copy(peer, me, r).start()
    send_cols_across(0, True)
    for r in every[1:]:
        send_cols_along(r, True)
        send_cols_across(r, True)
    for t in range(1, depth // 2):
        gs.across(plane_at(t))
    core_spread = send(packed, packed, r_send.at[1], r_recv.at[1], peer)

    @pl.when(sums)
    def _():
        for k in range(1, chips):
            spread(chip, chip_at(k)).wait_recv()
        core_spread.start()

    for t in range(depth // 2, depth):
        gs.across(plane_at(t))
    pl.when(bulk)(lambda: core_spread.wait_recv())
    spot = 0
    for a in range(BLOCKS):
        for b in range(a, BLOCKS):
            value = packed[pl.ds(spot * size, size), :]
            final[pl.ds(a * size, size), pl.ds(b * size, size)] = value
            if a != b:
                final[pl.ds(b * size, size), pl.ds(a * size, size)] = (
                    value.astype(jnp.float32).T.astype(jnp.bfloat16)
                )
            spot += 1
    for t in range(depth):
        gs.whole(plane_at(t))
    own_slab.wait()
    own_cols.wait()
    load_of.wait()

    strip = min(512, slab)
    for r, (start, count) in enumerate(SPLIT):
        for k in range(1, n):
            cols_copy(me, (me + k) % n, r).wait_recv()
        some = pl.ds(start * unit, count * unit)
        left = lax.dot_general(
            cols_ref[:, some], final[...], (((0,), (0,)), ((), ())),
            preferred_element_type=jnp.float32,
        ).astype(jnp.bfloat16)
        if r == len(SPLIT) - 1:
            left_ref[...] = left
            continue

        @pl.loop(0, slab // strip)
        def _(j):
            cs = rows(j * strip, strip)
            upd_ref[some, cs] = upd_ref[some, cs] + jnp.dot(
                left, slab_ref[:, cs], preferred_element_type=jnp.float32
            ) * (1.0 / tokens)

    gx.drain()
    gs.drain()
    for r in range(len(SPLIT)):
        for k in range(1, n):
            cols_copy((me + k) % n, me, r).wait_send()
    pl.when(bulk)(lambda: core_sum.wait_send())

    @pl.when(sums)
    def _():
        core_spread.wait_send()
        for k in range(1, chips):
            scatter(k, chip_at(k), chip).wait_send()
            spread(chip_at(k), chip).wait_send()


def exchange(n, x, f, g, of):
    sh, din = x.shape
    feat = f.shape[0]
    tokens, chips = n * sh, n // 2
    width, slab = g.shape[1] // n, of.shape[1]
    size = tokens // BLOCKS
    packed = PACKED * size
    bf, f32, dma = jnp.bfloat16, jnp.float32, pltpu.SemaphoreType.DMA
    last = SPLIT[-1][1] * (width // UNITS)
    scratch = [
        ((tokens, din), bf), (f.shape, bf), (g.shape, bf), ((tokens, width), bf),
        ((tokens, feat), bf), ((tokens, feat), bf),
        ((packed, size), f32), ((packed, size), f32), ((packed, size), bf),
        ((chips, packed // chips, size), bf), ((packed, size), bf), ((tokens, tokens), bf),
    ]
    used = sum(functools.reduce(lambda a, b: a * b, s) * jnp.dtype(t).itemsize for s, t in scratch)
    return pl.pallas_call(
        functools.partial(exchange_kernel, n),
        out_shape=(
            pltpu.VMEM(of.shape, of.dtype), pltpu.VMEM((tokens, slab), bf), pltpu.VMEM((last, tokens), bf),
        ),
        in_specs=[pl.BlockSpec(memory_space=pltpu.HBM)] * 4,
        out_specs=(pl.BlockSpec(memory_space=pltpu.VMEM),) * 3,
        scratch_shapes=[pltpu.VMEM(s, t) for s, t in scratch] + [
            dma((6,)), dma((n, 4)), dma((4, n)), dma((n, 2)), dma((4, n)),
            dma((len(SPLIT), n)), dma((len(SPLIT), n)), dma((2,)), dma((2,)),
            dma((chips,)), dma((chips,)), dma((chips,)), dma((chips,)),
        ],
        compiler_params=pltpu.CompilerParams(
            collective_id=0, has_side_effects=True, vmem_limit_bytes=used + 3 * 1024 * 1024
        ),
    )(*(pltpu.with_memory_space_constraint(v, pltpu.HBM) for v in (x, f, g, of)))


def write_kernel(parts, upd, slab_ref, left, dst, buf, sem, strip_sem):
    tokens, slab = slab_ref.shape
    ready = upd.shape[0] - left.shape[0]
    size = ready // parts
    strips, _, strip = buf.shape

    def copy(i):
        some = pl.ds(i * size, size)
        return pltpu.make_async_copy(upd.at[some, :], dst.at[some, :], sem.at[i])

    def strip_copy(j):
        return pltpu.make_async_copy(
            buf.at[j], dst.at[pl.ds(ready, left.shape[0]), pl.ds(j * strip, strip)], strip_sem.at[j]
        )

    for i in range(parts):
        copy(i).start()
    for j in range(strips):
        cs = pl.ds(j * strip, strip)
        buf[j] = upd[pl.ds(ready, left.shape[0]), cs] + jnp.dot(
            left[...], slab_ref[:, cs], preferred_element_type=jnp.float32
        ) * (1.0 / tokens)
        strip_copy(j).start()
    for i in range(parts):
        copy(i).wait()
    for j in range(strips):
        strip_copy(j).wait()


def write(upd, slab_ref, left):
    strip = min(512, upd.shape[1])
    strips, parts = upd.shape[1] // strip, 8
    return pl.pallas_call(
        functools.partial(write_kernel, parts),
        out_shape=jax.ShapeDtypeStruct(upd.shape, upd.dtype),
        in_specs=[pl.BlockSpec(memory_space=pltpu.VMEM)] * 3,
        out_specs=pl.BlockSpec(memory_space=pl.ANY),
        scratch_shapes=[
            pltpu.VMEM((strips, left.shape[0], strip), upd.dtype),
            pltpu.SemaphoreType.DMA((parts,)), pltpu.SemaphoreType.DMA((strips,)),
        ],
        compiler_params=pltpu.CompilerParams(vmem_limit_bytes=12 * 1024 * 1024),
    )(upd, slab_ref, left)


def per_device(n, inputs, input_factor, out_grads, output_factor):
    return write(*exchange(n, inputs, input_factor, out_grads, output_factor))


def solution(mesh):
    spec = P(("groups", "row"), None)
    return jax.shard_map(
        functools.partial(per_device, mesh.shape["row"]),
        mesh=mesh, in_specs=(spec,) * 4, out_specs=spec, check_vma=False,
    )
```

```python
import functools

import jax
import jax.numpy as jnp
from jax import lax
from jax.experimental import pallas as pl
from jax.experimental.pallas import tpu as pltpu
from jax.sharding import PartitionSpec as P

UP, DOWN, SIDE, CORE = range(4)
BLOCKS = 4
PACKED = BLOCKS * (BLOCKS + 1) // 2
SPLIT = ((0, 4),)
STRIP = 512
UNITS = 4


def exchange_kernel(
    n, x_ref, f_ref, g_ref, of_ref, upd_ref, slab_ref, left_ref,
    xall, fv, gv, cols_ref, proj, proj_low, part, in0, out1, in1, packed, final,
    local_sem, x_recv, x_send, s_recv, s_send, c_recv, c_send,
    r_recv, r_send, rs_recv, rs_send, ag_recv, ag_send,
):
    me = lax.axis_index("row")
    depth = n // 4
    z, y, c = me // 4, (me // 2) % 2, me % 2
    sh = x_ref.shape[0]
    tokens = n * sh
    slab = slab_ref.shape[1]
    width = cols_ref.shape[1]
    unit = width // UNITS
    feat = f_ref.shape[0]
    chips = n // 2
    chip = z * 2 + y
    half_way = chips // 2

    def index(zz, yy, cc):
        return zz * 4 + yy * 2 + cc

    side, peer = index(z, 1 - y, c), index(z, y, 1 - c)

    def rows(start, size):
        return pl.ds(pl.multiple_of(start, size), size)

    def is_end(zz):
        return (zz == 0) | (zz == depth - 1)

    load_f = pltpu.make_async_copy(f_ref, fv, local_sem.at[0])
    load_x = pltpu.make_async_copy(x_ref, xall.at[rows(me * sh, sh), :], local_sem.at[1])
    load_g = pltpu.make_async_copy(g_ref, gv, local_sem.at[2])
    load_of = pltpu.make_async_copy(of_ref, upd_ref, local_sem.at[5])
    load_x.start()
    load_g.start()
    load_f.start()

    barrier = pltpu.get_barrier_semaphore()
    for k in range(1, n):
        pl.semaphore_signal(
            barrier, inc=1, device_id={"row": (me + k) % n}, device_id_type=pl.DeviceIdType.MESH
        )
    pl.semaphore_wait(barrier, n - 1)

    def send(src, dst, send_sem, recv_sem, target):
        return pltpu.make_async_remote_copy(
            src_ref=src, dst_ref=dst, send_sem=send_sem, recv_sem=recv_sem,
            device_id={"row": target}, device_id_type=pl.DeviceIdType.MESH,
        )

    class Gather:
        def __init__(self, buf, recv, sems, pieces, groups, windowed):
            self.buf, self.recv, self.sems = buf, recv, sems
            self.pieces, self.groups, self.windowed = pieces, groups, windowed
            self.width = buf.shape[1] // pieces
            self.size = pieces // groups
            self.end_near = half_way if windowed else pieces
            self.mid_near = min(half_way + 1, pieces) if windowed else pieces
            self.end_along = min(self.end_near + 1, pieces) if windowed else pieces

        def along_takes(self, zz, p):
            if not self.windowed:
                return True
            return jnp.logical_not(is_end(zz)) | ((p - 2 * zz + self.pieces) % self.pieces < self.end_along)

        def near_takes(self, cc, p):
            if not self.windowed:
                return True
            reach = jnp.where(is_end(z), self.end_near, self.mid_near)
            return (p - cc + self.pieces) % self.pieces < reach

        def copy(self, origin, kind, target, first, count, group, src=None):
            cols = pl.ds(pl.multiple_of(first * self.width, self.width), count * self.width)
            view = self.buf.at[rows(origin * sh, sh), cols]
            return send(
                view if src is None else src.at[:, cols], view,
                self.sems.at[kind, origin], self.recv.at[origin, group], target,
            )

        def when(self, gate, fn):
            if gate is True:
                fn()
            else:
                pl.when(gate)(fn)

        def along(self, origin, kind, group, src=None):
            to = z + 1 if kind == UP else z - 1
            for i in range(self.size):
                p = group * self.size + i
                self.when(self.along_takes(to, p), lambda: self.copy(
                    origin, kind, index(to, y, c), p, 1, group, src).start())

        def detours(self, plane):
            if self.windowed or depth < 4:
                return False
            return ((z == 1) & (plane == 0)) | ((z == depth - 2) & (plane == depth - 1))

        def near_by(self, origin, group, src=None):
            detour = self.detours(origin // 4)
            for i in range(self.size):
                p = group * self.size + i
                takes = self.near_takes(z * 2 + 1 - y, p)
                if detour is not False:
                    takes = jnp.logical_not(detour)
                self.when(takes, lambda: self.copy(
                    origin, SIDE, side, p, 1, 0, src).start())
                self.when(self.near_takes(chip, p), lambda: self.copy(
                    origin, CORE, peer, p, 1, 0, src).start())

        def each(self, fn):
            if self.groups == 1:
                fn(0)
            else:
                pl.loop(0, self.groups)(fn)

        def own_along(self, src=None, hops=None):
            def go(group):
                @pl.when((z + 1 < depth) & (True if hops is None else z == hops))
                def _():
                    self.along(me, UP, group, src)

                @pl.when((z > 0) & (True if hops is None else depth - 1 - z == hops))
                def _():
                    self.along(me, DOWN, group, src)

            self.each(go)

        def own_near(self, src=None):
            self.each(lambda group: self.near_by(me, group, src))

        def came(self, origin, group):
            def take(count):
                self.copy(origin, CORE, peer, 0, count, group).wait_recv()

            if not self.windowed:
                take(self.size)
                return
            got = sum(
                self.along_takes(z, group * self.size + i).astype(jnp.int32) for i in range(self.size)
            )
            for count in range(1, self.size + 1):
                pl.when(got == count)(functools.partial(take, count))

        def column(self, k, near=True):
            def go(group):
                @pl.when(z - k >= 0)
                def _():
                    origin = index(z - k, y, c)
                    self.came(origin, group)

                    @pl.when(z + 1 < depth)
                    def _():
                        self.along(origin, UP, group)

                    if near:
                        self.near_by(origin, group)

                @pl.when(z + k < depth)
                def _():
                    origin = index(z + k, y, c)
                    self.came(origin, group)

                    @pl.when(z > 0)
                    def _():
                        self.along(origin, DOWN, group)

                    if near:
                        self.near_by(origin, group)

            self.each(go)

        def column_near(self, k):
            def go(group):
                @pl.when(z - k >= 0)
                def _():
                    self.near_by(index(z - k, y, c), group)

                @pl.when(z + k < depth)
                def _():
                    self.near_by(index(z + k, y, c), group)

            self.each(go)

        def by_end(self, fn):
            if self.end_near == self.mid_near:
                fn(self.end_near)
            else:
                pl.when(is_end(z))(functools.partial(fn, self.end_near))
                pl.when(jnp.logical_not(is_end(z)))(functools.partial(fn, self.mid_near))

        def across(self, plane):
            origin = index(plane, 1 - y, c)
            self.by_end(lambda count: self.copy(origin, CORE, peer, 0, count, 0).wait_recv())

            def go(group):
                for i in range(self.size):
                    p = group * self.size + i
                    self.when(self.near_takes(chip, p), lambda: self.copy(
                        origin, CORE, peer, p, 1, 0).start())

            self.each(go)
            if self.detours(plane) is False:
                return

            @pl.when((plane == z) & (z == 0))
            def _():
                self.copy(origin, UP, index(1, y, c), 0, self.pieces, 0).start()

            @pl.when((plane == z) & (z == depth - 1))
            def _():
                self.copy(origin, DOWN, index(depth - 2, y, c), 0, self.pieces, 0).start()

        def whole(self, plane):
            def take(count):
                self.copy(index(plane, 0, 1 - c), CORE, peer, 0, count, 0).wait_recv()
                self.copy(index(plane, 1, 1 - c), CORE, peer, 0, count, 0).wait_recv()

            self.by_end(take)

        def drain(self):
            def sent(origin, kind, count):
                self.copy(origin, kind, peer, 0, count, 0).wait_send()

            for plane in range(depth):
                origin = index(plane, y, c)
                for kind, to, gate in (
                    (UP, z + 1, (plane <= z) & (z + 1 < depth)),
                    (DOWN, z - 1, (plane >= z) & (z > 0)),
                ):
                    if self.end_along == self.pieces:
                        pl.when(gate)(functools.partial(sent, origin, kind, self.pieces))
                    else:
                        pl.when(gate & is_end(to))(functools.partial(sent, origin, kind, self.end_along))
                        pl.when(gate & jnp.logical_not(is_end(to)))(
                            functools.partial(sent, origin, kind, self.pieces))

                def near(count, origin=origin, plane=plane):
                    detour = self.detours(plane)
                    if detour is False:
                        sent(origin, SIDE, count)
                    else:
                        pl.when(jnp.logical_not(detour))(functools.partial(sent, origin, SIDE, count))
                    sent(origin, CORE, count)
                    sent(index(plane, 1 - y, c), CORE, count)

                self.by_end(near)
            if self.detours(z) is False:
                return
            other = index(z, 1 - y, c)
            pl.when(z == 0)(functools.partial(sent, other, UP, self.pieces))
            pl.when(z == depth - 1)(functools.partial(sent, other, DOWN, self.pieces))

    gx = Gather(xall, x_recv, x_send, chips, 4, True)
    gs = Gather(slab_ref, s_recv, s_send, 2, 2, False)
    gx.own_along(x_ref)
    gx.own_near(x_ref)

    flip = z >= (depth + 1) // 2
    zm = jnp.where(flip, depth - 1 - z, z)

    def plane_at(t):
        near = zm - (t + 1) // 2 if t % 2 else zm + t // 2
        p = jnp.where(t <= 2 * zm, near, t)
        return jnp.where(flip, depth - 1 - p, p)

    block = 4 * sh
    tile = min(256, feat)
    far = (z + depth // 2) % depth
    far_weight = jnp.where(is_end(far), 1.0, 0.5).astype(jnp.float32)

    def project(plane):
        xs = rows(plane * block, block)

        def body(reach):
            @pl.loop(0, feat // tile)
            def _(j):
                fs = rows(j * tile, tile)
                value = jnp.zeros((block, tile), jnp.float32)
                for k in range(reach):
                    cs = rows((chip + k) % chips * (2 * feat), 2 * feat)
                    term = lax.dot_general(
                        xall[xs, cs], fv[fs, cs], (((1,), (1,)), ((), ())),
                        preferred_element_type=jnp.float32,
                    )
                    if k == 0:
                        term = term * 0.5
                    elif k == half_way:
                        term = term * far_weight
                    value = value + term
                high = value.astype(jnp.bfloat16)
                proj[xs, fs] = high
                proj_low[xs, fs] = (value - high.astype(jnp.float32)).astype(jnp.bfloat16)

        gx.by_end(body)

    def cols_copy(d, origin, r):
        start, count = SPLIT[r]
        return send(
            gv.at[:, pl.ds(pl.multiple_of(d * width + start * unit, unit), count * unit)],
            cols_ref.at[rows(origin * sh, sh), pl.ds(start * unit, count * unit)],
            c_send.at[r, d], c_recv.at[r, origin], d,
        )

    every = range(len(SPLIT))
    beside = (z == 1) | (z == depth - 2)
    close = jnp.where(z == 1, 0, depth - 1)

    def send_cols_to(r, zz, yy):
        for cc in range(2):
            cols_copy(index(zz, yy, cc), me, r).start()

    def send_cols_along(r, ends):
        @pl.loop(1, depth)
        def _(k):
            zz = (z + k) % depth

            @pl.when((is_end(zz) == ends) & jnp.logical_not(beside & (zz == close)))
            def _():
                send_cols_to(r, zz, y)

    def send_cols_close():
        @pl.when(beside)
        def _():
            for r in every:
                send_cols_to(r, close, y)

    def send_cols_side(r):
        send_cols_to(r, z, 1 - y)

    def send_cols_across(r, ends):
        if not ends:
            pl.when(jnp.logical_not(is_end(z)))(lambda: send_cols_side(r))

        @pl.loop(1, depth)
        def _(k):
            zz = (z + k) % depth
            pl.when(is_end(zz) == ends)(lambda: send_cols_to(r, zz, 1 - y))

    load_x.wait()
    load_g.wait()
    own_slab = pltpu.make_async_copy(
        gv.at[:, pl.ds(0, slab)], slab_ref.at[rows(me * sh, sh), :], local_sem.at[3]
    )
    own_cols = pltpu.make_async_copy(
        gv.at[:, rows(me * width, width)], cols_ref.at[rows(me * sh, sh), :], local_sem.at[4]
    )
    own_slab.start()
    own_cols.start()
    slab_src = gv.at[:, pl.ds(0, slab)]
    end, middle = is_end(z), jnp.logical_not(is_end(z))
    gs.own_along(slab_src, 0)

    @pl.when(end)
    def _():
        gs.own_near(slab_src)
        for r in every:
            send_cols_side(r)

    load_f.wait()
    load_of.start()
    for k in range(1, depth):
        gx.column(k)
        gs.own_along(slab_src, k)
        if k == 1:
            send_cols_close()
        if k == max(1, depth - 2):
            pl.when(middle)(lambda: gs.own_near(slab_src))
        plane = plane_at(k - 1)
        gx.across(plane)
        gx.whole(plane)
        project(plane)
        if k == 1:
            pl.when(end)(lambda: gs.across(z))

    gs.column(1)
    plane = plane_at(depth - 1)
    gx.across(plane)
    gx.whole(plane)
    project(plane)

    own_features = rows(me * feat, feat)
    size = tokens // BLOCKS
    share = PACKED * size // chips

    spot = 0
    for a in range(BLOCKS):
        some, rest = pl.ds(a * size, size), pl.ds(a * size, tokens - a * size)
        total = jnp.zeros((size, tokens - a * size), jnp.float32)
        for piece in (proj, proj_low):
            for lhs, rhs in ((piece[some, :], xall[rest, own_features]), (xall[some, own_features], piece[rest, :])):
                total = total + lax.dot_general(
                    lhs, rhs, (((1,), (1,)), ((), ())), preferred_element_type=jnp.float32
                )
        for j in range(BLOCKS - a):
            part[pl.ds((spot + j) * size, size), :] = total[:, j * size:(j + 1) * size]
        spot += BLOCKS - a

    sums, bulk = c == 1, c == 0
    core_sum = send(part, in0, r_send.at[0], r_recv.at[0], peer)
    pl.when(bulk)(lambda: core_sum.start())

    def chip_at(k):
        return (chip + k) % chips

    def device_of(other):
        return index(other // 2, other % 2, c)

    def scatter(k, other, slot):
        return send(
            out1.at[rows(other * share, share), :], in1.at[slot],
            rs_send.at[other], rs_recv.at[slot], device_of(other),
        )

    def spread(other, origin):
        view = packed.at[rows(origin * share, share), :]
        return send(view, view, ag_send.at[other], ag_recv.at[origin], device_of(other))

    @pl.when(sums)
    def _():
        core_sum.wait_recv()
        out1[...] = (part[...] + in0[...]).astype(jnp.bfloat16)
        for k in range(1, chips):
            scatter(k, chip_at(k), chip).start()

    @pl.when(bulk)
    def _():
        for r in every:
            send_cols_along(r, False)

    for k in range(2, min(3, depth)):
        gs.column(k)

    @pl.when(sums)
    def _():
        mine = rows(chip * share, share)
        total = part[mine, :] + in0[mine, :]
        for k in range(1, chips):
            scatter(k, chip_at(k), chip_at(k)).wait_recv()
            total = total + in1[chip_at(k)].astype(jnp.float32)
        packed[mine, :] = (total * float(n * feat) ** (-0.5)).astype(jnp.bfloat16)
        for k in range(1, chips):
            spread(chip_at(k), chip).start()
        for r in every:
            send_cols_along(r, False)

    for k in range(3, depth):
        gs.column(k)
    for r in every:
        send_cols_across(r, False)
    send_cols_along(0, True)
    pl.when(middle)(lambda: gs.across(z))
    for r in every:
        cols_copy(peer, me, r).start()
    send_cols_across(0, True)
    for r in every[1:]:
        send_cols_along(r, True)
        send_cols_across(r, True)
    for t in range(1, depth // 2):
        gs.across(plane_at(t))
    core_spread = send(packed, packed, r_send.at[1], r_recv.at[1], peer)

    @pl.when(sums)
    def _():
        for k in range(1, chips):
            spread(chip, chip_at(k)).wait_recv()
        core_spread.start()

    for t in range(depth // 2, depth):
        gs.across(plane_at(t))
    pl.when(bulk)(lambda: core_spread.wait_recv())
    spot = 0
    for a in range(BLOCKS):
        for b in range(a, BLOCKS):
            value = packed[pl.ds(spot * size, size), :]
            final[pl.ds(a * size, size), pl.ds(b * size, size)] = value
            if a != b:
                final[pl.ds(b * size, size), pl.ds(a * size, size)] = (
                    value.astype(jnp.float32).T.astype(jnp.bfloat16)
                )
            spot += 1
    for t in range(depth):
        gs.whole(plane_at(t))
    own_slab.wait()
    own_cols.wait()
    load_of.wait()

    for r, (start, count) in enumerate(SPLIT):
        for k in range(1, n):
            cols_copy(me, (me + k) % n, r).wait_recv()
        some = pl.ds(start * unit, count * unit)
        left_ref[some, :] = lax.dot_general(
            cols_ref[:, some], final[...], (((0,), (0,)), ((), ())),
            preferred_element_type=jnp.float32,
        ).astype(jnp.bfloat16)

    gx.drain()
    gs.drain()
    for r in range(len(SPLIT)):
        for k in range(1, n):
            cols_copy((me + k) % n, me, r).wait_send()
    pl.when(bulk)(lambda: core_sum.wait_send())

    @pl.when(sums)
    def _():
        core_spread.wait_send()
        for k in range(1, chips):
            scatter(k, chip_at(k), chip).wait_send()
            spread(chip_at(k), chip).wait_send()


def exchange(n, x, f, g, of):
    sh, din = x.shape
    feat = f.shape[0]
    tokens, chips = n * sh, n // 2
    width, slab = g.shape[1] // n, of.shape[1]
    size = tokens // BLOCKS
    packed = PACKED * size
    bf, f32, dma = jnp.bfloat16, jnp.float32, pltpu.SemaphoreType.DMA
    scratch = [
        ((tokens, din), bf), (f.shape, bf), (g.shape, bf), ((tokens, width), bf),
        ((tokens, feat), bf), ((tokens, feat), bf),
        ((packed, size), f32), ((packed, size), f32), ((packed, size), bf),
        ((chips, packed // chips, size), bf), ((packed, size), bf), ((tokens, tokens), bf),
    ]
    used = sum(functools.reduce(lambda a, b: a * b, s) * jnp.dtype(t).itemsize for s, t in scratch)
    return pl.pallas_call(
        functools.partial(exchange_kernel, n),
        out_shape=(
            pltpu.VMEM(of.shape, of.dtype), pltpu.VMEM((tokens, slab), bf), pltpu.VMEM((width, tokens), bf),
        ),
        in_specs=[pl.BlockSpec(memory_space=pltpu.HBM)] * 4,
        out_specs=(pl.BlockSpec(memory_space=pltpu.VMEM),) * 3,
        scratch_shapes=[pltpu.VMEM(s, t) for s, t in scratch] + [
            dma((6,)), dma((n, 4)), dma((4, n)), dma((n, 2)), dma((4, n)),
            dma((len(SPLIT), n)), dma((len(SPLIT), n)), dma((2,)), dma((2,)),
            dma((chips,)), dma((chips,)), dma((chips,)), dma((chips,)),
        ],
        compiler_params=pltpu.CompilerParams(
            collective_id=0, has_side_effects=True, vmem_limit_bytes=used + 3 * 1024 * 1024
        ),
    )(*(pltpu.with_memory_space_constraint(v, pltpu.HBM) for v in (x, f, g, of)))


def write_kernel(upd, slab_ref, left, dst, buf, sem):
    tokens, slab = slab_ref.shape
    slots, _, strip = buf.shape
    strips = slab // strip

    def copy(j):
        return pltpu.make_async_copy(
            buf.at[j % slots], dst.at[:, pl.ds(j * strip, strip)], sem.at[j % slots]
        )

    for j in range(strips):
        cs = pl.ds(j * strip, strip)
        if j >= slots:
            copy(j - slots).wait()
        buf[j % slots] = upd[:, cs] + jnp.dot(
            left[...], slab_ref[:, cs], preferred_element_type=jnp.float32
        ) * (1.0 / tokens)
        copy(j).start()
    for j in range(max(0, strips - slots), strips):
        copy(j).wait()


def write(upd, slab_ref, left):
    strip = min(STRIP, upd.shape[1])
    slots = min(upd.shape[1] // strip, 4)
    return pl.pallas_call(
        write_kernel,
        out_shape=jax.ShapeDtypeStruct(upd.shape, upd.dtype),
        in_specs=[pl.BlockSpec(memory_space=pltpu.VMEM)] * 3,
        out_specs=pl.BlockSpec(memory_space=pl.ANY),
        scratch_shapes=[
            pltpu.VMEM((slots, upd.shape[0], strip), upd.dtype), pltpu.SemaphoreType.DMA((slots,)),
        ],
        compiler_params=pltpu.CompilerParams(vmem_limit_bytes=slots * upd.shape[0] * strip * 4 + 2 * 1024 * 1024),
    )(upd, slab_ref, left)


def per_device(n, inputs, input_factor, out_grads, output_factor):
    return write(*exchange(n, inputs, input_factor, out_grads, output_factor))


def solution(mesh):
    spec = P(("groups", "row"), None)
    return jax.shard_map(
        functools.partial(per_device, mesh.shape["row"]),
        mesh=mesh, in_specs=(spec,) * 4, out_specs=spec, check_vma=False,
    )
```

```python
import functools

import jax
import jax.numpy as jnp
from jax import lax
from jax.experimental import pallas as pl
from jax.experimental.pallas import tpu as pltpu
from jax.sharding import PartitionSpec as P

UP, DOWN, SIDE, CORE = range(4)
BLOCKS = 4
PACKED = BLOCKS * (BLOCKS + 1) // 2
SPLIT = ((0, 4),)
STRIP = 1024
UNITS = 4


def exchange_kernel(
    n, x_ref, f_ref, g_ref, of_ref, upd_ref, slab_ref, left_ref,
    xall, fv, gv, cols_ref, proj, proj_low, part, in0, out1, in1, packed, final,
    local_sem, x_recv, x_send, s_recv, s_send, c_recv, c_send,
    r_recv, r_send, rs_recv, rs_send, ag_recv, ag_send,
):
    me = lax.axis_index("row")
    depth = n // 4
    z, y, c = me // 4, (me // 2) % 2, me % 2
    sh = x_ref.shape[0]
    tokens = n * sh
    slab = slab_ref.shape[1]
    width = cols_ref.shape[1]
    unit = width // UNITS
    feat = f_ref.shape[0]
    chips = n // 2
    chip = z * 2 + y
    half_way = chips // 2

    def index(zz, yy, cc):
        return zz * 4 + yy * 2 + cc

    side, peer = index(z, 1 - y, c), index(z, y, 1 - c)

    def rows(start, size):
        return pl.ds(pl.multiple_of(start, size), size)

    def is_end(zz):
        return (zz == 0) | (zz == depth - 1)

    load_f = pltpu.make_async_copy(f_ref, fv, local_sem.at[0])
    load_x = pltpu.make_async_copy(x_ref, xall.at[rows(me * sh, sh), :], local_sem.at[1])
    load_g = pltpu.make_async_copy(g_ref, gv, local_sem.at[2])
    load_of = pltpu.make_async_copy(of_ref, upd_ref, local_sem.at[5])
    load_x.start()
    load_g.start()
    load_f.start()

    barrier = pltpu.get_barrier_semaphore()
    for k in range(1, n):
        pl.semaphore_signal(
            barrier, inc=1, device_id={"row": (me + k) % n}, device_id_type=pl.DeviceIdType.MESH
        )
    pl.semaphore_wait(barrier, n - 1)

    def send(src, dst, send_sem, recv_sem, target):
        return pltpu.make_async_remote_copy(
            src_ref=src, dst_ref=dst, send_sem=send_sem, recv_sem=recv_sem,
            device_id={"row": target}, device_id_type=pl.DeviceIdType.MESH,
        )

    class Gather:
        def __init__(self, buf, recv, sems, pieces, groups, windowed):
            self.buf, self.recv, self.sems = buf, recv, sems
            self.pieces, self.groups, self.windowed = pieces, groups, windowed
            self.width = buf.shape[1] // pieces
            self.size = pieces // groups
            self.end_near = half_way if windowed else pieces
            self.mid_near = min(half_way + 1, pieces) if windowed else pieces
            self.end_along = min(self.end_near + 1, pieces) if windowed else pieces

        def along_takes(self, zz, p):
            if not self.windowed:
                return True
            return jnp.logical_not(is_end(zz)) | ((p - 2 * zz + self.pieces) % self.pieces < self.end_along)

        def near_takes(self, cc, p):
            if not self.windowed:
                return True
            reach = jnp.where(is_end(z), self.end_near, self.mid_near)
            return (p - cc + self.pieces) % self.pieces < reach

        def copy(self, origin, kind, target, first, count, group, src=None):
            cols = pl.ds(pl.multiple_of(first * self.width, self.width), count * self.width)
            view = self.buf.at[rows(origin * sh, sh), cols]
            return send(
                view if src is None else src.at[:, cols], view,
                self.sems.at[kind, origin], self.recv.at[origin, group], target,
            )

        def when(self, gate, fn):
            if gate is True:
                fn()
            else:
                pl.when(gate)(fn)

        def along(self, origin, kind, group, src=None):
            to = z + 1 if kind == UP else z - 1
            for i in range(self.size):
                p = group * self.size + i
                self.when(self.along_takes(to, p), lambda: self.copy(
                    origin, kind, index(to, y, c), p, 1, group, src).start())

        def detours(self, plane):
            if self.windowed or depth < 4:
                return False
            return ((z == 1) & (plane == 0)) | ((z == depth - 2) & (plane == depth - 1))

        def near_by(self, origin, group, src=None):
            detour = self.detours(origin // 4)
            for i in range(self.size):
                p = group * self.size + i
                takes = self.near_takes(z * 2 + 1 - y, p)
                if detour is not False:
                    takes = jnp.logical_not(detour)
                self.when(takes, lambda: self.copy(
                    origin, SIDE, side, p, 1, 0, src).start())
                self.when(self.near_takes(chip, p), lambda: self.copy(
                    origin, CORE, peer, p, 1, 0, src).start())

        def each(self, fn):
            if self.groups == 1:
                fn(0)
            else:
                pl.loop(0, self.groups)(fn)

        def own_along(self, src=None, hops=None):
            def go(group):
                @pl.when((z + 1 < depth) & (True if hops is None else z == hops))
                def _():
                    self.along(me, UP, group, src)

                @pl.when((z > 0) & (True if hops is None else depth - 1 - z == hops))
                def _():
                    self.along(me, DOWN, group, src)

            self.each(go)

        def own_near(self, src=None):
            self.each(lambda group: self.near_by(me, group, src))

        def came(self, origin, group):
            def take(count):
                self.copy(origin, CORE, peer, 0, count, group).wait_recv()

            if not self.windowed:
                take(self.size)
                return
            got = sum(
                self.along_takes(z, group * self.size + i).astype(jnp.int32) for i in range(self.size)
            )
            for count in range(1, self.size + 1):
                pl.when(got == count)(functools.partial(take, count))

        def column(self, k, near=True):
            def go(group):
                @pl.when(z - k >= 0)
                def _():
                    origin = index(z - k, y, c)
                    self.came(origin, group)

                    @pl.when(z + 1 < depth)
                    def _():
                        self.along(origin, UP, group)

                    if near:
                        self.near_by(origin, group)

                @pl.when(z + k < depth)
                def _():
                    origin = index(z + k, y, c)
                    self.came(origin, group)

                    @pl.when(z > 0)
                    def _():
                        self.along(origin, DOWN, group)

                    if near:
                        self.near_by(origin, group)

            self.each(go)

        def column_near(self, k):
            def go(group):
                @pl.when(z - k >= 0)
                def _():
                    self.near_by(index(z - k, y, c), group)

                @pl.when(z + k < depth)
                def _():
                    self.near_by(index(z + k, y, c), group)

            self.each(go)

        def by_end(self, fn):
            if self.end_near == self.mid_near:
                fn(self.end_near)
            else:
                pl.when(is_end(z))(functools.partial(fn, self.end_near))
                pl.when(jnp.logical_not(is_end(z)))(functools.partial(fn, self.mid_near))

        def across(self, plane):
            origin = index(plane, 1 - y, c)
            self.by_end(lambda count: self.copy(origin, CORE, peer, 0, count, 0).wait_recv())

            def go(group):
                for i in range(self.size):
                    p = group * self.size + i
                    self.when(self.near_takes(chip, p), lambda: self.copy(
                        origin, CORE, peer, p, 1, 0).start())

            self.each(go)
            if self.detours(plane) is False:
                return

            @pl.when((plane == z) & (z == 0))
            def _():
                self.copy(origin, UP, index(1, y, c), 0, self.pieces, 0).start()

            @pl.when((plane == z) & (z == depth - 1))
            def _():
                self.copy(origin, DOWN, index(depth - 2, y, c), 0, self.pieces, 0).start()

        def whole(self, plane):
            def take(count):
                self.copy(index(plane, 0, 1 - c), CORE, peer, 0, count, 0).wait_recv()
                self.copy(index(plane, 1, 1 - c), CORE, peer, 0, count, 0).wait_recv()

            self.by_end(take)

        def drain(self):
            def sent(origin, kind, count):
                self.copy(origin, kind, peer, 0, count, 0).wait_send()

            for plane in range(depth):
                origin = index(plane, y, c)
                for kind, to, gate in (
                    (UP, z + 1, (plane <= z) & (z + 1 < depth)),
                    (DOWN, z - 1, (plane >= z) & (z > 0)),
                ):
                    if self.end_along == self.pieces:
                        pl.when(gate)(functools.partial(sent, origin, kind, self.pieces))
                    else:
                        pl.when(gate & is_end(to))(functools.partial(sent, origin, kind, self.end_along))
                        pl.when(gate & jnp.logical_not(is_end(to)))(
                            functools.partial(sent, origin, kind, self.pieces))

                def near(count, origin=origin, plane=plane):
                    detour = self.detours(plane)
                    if detour is False:
                        sent(origin, SIDE, count)
                    else:
                        pl.when(jnp.logical_not(detour))(functools.partial(sent, origin, SIDE, count))
                    sent(origin, CORE, count)
                    sent(index(plane, 1 - y, c), CORE, count)

                self.by_end(near)
            if self.detours(z) is False:
                return
            other = index(z, 1 - y, c)
            pl.when(z == 0)(functools.partial(sent, other, UP, self.pieces))
            pl.when(z == depth - 1)(functools.partial(sent, other, DOWN, self.pieces))

    gx = Gather(xall, x_recv, x_send, chips, 4, True)
    gs = Gather(slab_ref, s_recv, s_send, 2, 2, False)
    gx.own_along(x_ref)
    gx.own_near(x_ref)

    flip = z >= (depth + 1) // 2
    zm = jnp.where(flip, depth - 1 - z, z)

    def plane_at(t):
        near = zm - (t + 1) // 2 if t % 2 else zm + t // 2
        p = jnp.where(t <= 2 * zm, near, t)
        return jnp.where(flip, depth - 1 - p, p)

    block = 4 * sh
    tile = min(256, feat)
    far = (z + depth // 2) % depth
    far_weight = jnp.where(is_end(far), 1.0, 0.5).astype(jnp.float32)

    def project(plane):
        xs = rows(plane * block, block)

        def body(reach):
            @pl.loop(0, feat // tile)
            def _(j):
                fs = rows(j * tile, tile)
                value = jnp.zeros((block, tile), jnp.float32)
                for k in range(reach):
                    cs = rows((chip + k) % chips * (2 * feat), 2 * feat)
                    term = lax.dot_general(
                        xall[xs, cs], fv[fs, cs], (((1,), (1,)), ((), ())),
                        preferred_element_type=jnp.float32,
                    )
                    if k == 0:
                        term = term * 0.5
                    elif k == half_way:
                        term = term * far_weight
                    value = value + term
                high = value.astype(jnp.bfloat16)
                proj[xs, fs] = high
                proj_low[xs, fs] = (value - high.astype(jnp.float32)).astype(jnp.bfloat16)

        gx.by_end(body)

    def cols_copy(d, origin, r):
        start, count = SPLIT[r]
        return send(
            gv.at[:, pl.ds(pl.multiple_of(d * width + start * unit, unit), count * unit)],
            cols_ref.at[rows(origin * sh, sh), pl.ds(start * unit, count * unit)],
            c_send.at[r, d], c_recv.at[r, origin], d,
        )

    every = range(len(SPLIT))
    beside = (z == 1) | (z == depth - 2)
    close = jnp.where(z == 1, 0, depth - 1)

    def send_cols_to(r, zz, yy):
        for cc in range(2):
            cols_copy(index(zz, yy, cc), me, r).start()

    def send_cols_along(r, ends):
        @pl.loop(1, depth)
        def _(k):
            zz = (z + k) % depth

            @pl.when((is_end(zz) == ends) & jnp.logical_not(beside & (zz == close)))
            def _():
                send_cols_to(r, zz, y)

    def send_cols_close():
        @pl.when(beside)
        def _():
            for r in every:
                send_cols_to(r, close, y)

    def send_cols_side(r):
        send_cols_to(r, z, 1 - y)

    def send_cols_across(r, ends):
        if not ends:
            pl.when(jnp.logical_not(is_end(z)))(lambda: send_cols_side(r))

        @pl.loop(1, depth)
        def _(k):
            zz = (z + k) % depth
            pl.when(is_end(zz) == ends)(lambda: send_cols_to(r, zz, 1 - y))

    load_x.wait()
    load_g.wait()
    own_slab = pltpu.make_async_copy(
        gv.at[:, pl.ds(0, slab)], slab_ref.at[rows(me * sh, sh), :], local_sem.at[3]
    )
    own_cols = pltpu.make_async_copy(
        gv.at[:, rows(me * width, width)], cols_ref.at[rows(me * sh, sh), :], local_sem.at[4]
    )
    own_slab.start()
    own_cols.start()
    slab_src = gv.at[:, pl.ds(0, slab)]
    end, middle = is_end(z), jnp.logical_not(is_end(z))
    gs.own_along(slab_src, 0)

    @pl.when(end)
    def _():
        gs.own_near(slab_src)
        for r in every:
            send_cols_side(r)

    load_f.wait()
    load_of.start()
    for k in range(1, depth):
        gx.column(k)
        gs.own_along(slab_src, k)
        if k == 1:
            send_cols_close()
        if k == max(1, depth - 2):
            pl.when(middle)(lambda: gs.own_near(slab_src))
        plane = plane_at(k - 1)
        gx.across(plane)
        gx.whole(plane)
        project(plane)
        if k == 1:
            pl.when(end)(lambda: gs.across(z))

    gs.column(1)
    plane = plane_at(depth - 1)
    gx.across(plane)
    gx.whole(plane)
    project(plane)

    own_features = rows(me * feat, feat)
    size = tokens // BLOCKS
    share = PACKED * size // chips

    spot = 0
    for a in range(BLOCKS):
        some, rest = pl.ds(a * size, size), pl.ds(a * size, tokens - a * size)
        total = jnp.zeros((size, tokens - a * size), jnp.float32)
        for piece in (proj, proj_low):
            for lhs, rhs in ((piece[some, :], xall[rest, own_features]), (xall[some, own_features], piece[rest, :])):
                total = total + lax.dot_general(
                    lhs, rhs, (((1,), (1,)), ((), ())), preferred_element_type=jnp.float32
                )
        for j in range(BLOCKS - a):
            part[pl.ds((spot + j) * size, size), :] = total[:, j * size:(j + 1) * size]
        spot += BLOCKS - a

    sums, bulk = c == 1, c == 0
    core_sum = send(part, in0, r_send.at[0], r_recv.at[0], peer)
    pl.when(bulk)(lambda: core_sum.start())

    def chip_at(k):
        return (chip + k) % chips

    def device_of(other):
        return index(other // 2, other % 2, c)

    def scatter(k, other, slot):
        return send(
            out1.at[rows(other * share, share), :], in1.at[slot],
            rs_send.at[other], rs_recv.at[slot], device_of(other),
        )

    def spread(other, origin):
        view = packed.at[rows(origin * share, share), :]
        return send(view, view, ag_send.at[other], ag_recv.at[origin], device_of(other))

    @pl.when(sums)
    def _():
        core_sum.wait_recv()
        out1[...] = (part[...] + in0[...]).astype(jnp.bfloat16)
        for k in range(1, chips):
            scatter(k, chip_at(k), chip).start()

    @pl.when(bulk)
    def _():
        for r in every:
            send_cols_along(r, False)

    for k in range(2, min(3, depth)):
        gs.column(k)

    @pl.when(sums)
    def _():
        mine = rows(chip * share, share)
        total = part[mine, :] + in0[mine, :]
        for k in range(1, chips):
            scatter(k, chip_at(k), chip_at(k)).wait_recv()
            total = total + in1[chip_at(k)].astype(jnp.float32)
        packed[mine, :] = (total * float(n * feat) ** (-0.5)).astype(jnp.bfloat16)
        for k in range(1, chips):
            spread(chip_at(k), chip).start()
        for r in every:
            send_cols_along(r, False)

    for k in range(3, depth):
        gs.column(k)
    for r in every:
        send_cols_across(r, False)
    send_cols_along(0, True)
    pl.when(middle)(lambda: gs.across(z))
    for r in every:
        cols_copy(peer, me, r).start()
    send_cols_across(0, True)
    for r in every[1:]:
        send_cols_along(r, True)
        send_cols_across(r, True)
    for t in range(1, depth // 2):
        gs.across(plane_at(t))
    core_spread = send(packed, packed, r_send.at[1], r_recv.at[1], peer)

    @pl.when(sums)
    def _():
        for k in range(1, chips):
            spread(chip, chip_at(k)).wait_recv()
        core_spread.start()

    for t in range(depth // 2, depth):
        gs.across(plane_at(t))
    pl.when(bulk)(lambda: core_spread.wait_recv())
    spot = 0
    for a in range(BLOCKS):
        for b in range(a, BLOCKS):
            value = packed[pl.ds(spot * size, size), :]
            final[pl.ds(a * size, size), pl.ds(b * size, size)] = value
            if a != b:
                final[pl.ds(b * size, size), pl.ds(a * size, size)] = (
                    value.astype(jnp.float32).T.astype(jnp.bfloat16)
                )
            spot += 1
    for t in range(depth):
        gs.whole(plane_at(t))
    own_slab.wait()
    own_cols.wait()
    load_of.wait()

    for r, (start, count) in enumerate(SPLIT):
        for k in range(1, n):
            cols_copy(me, (me + k) % n, r).wait_recv()
        some = pl.ds(start * unit, count * unit)
        left_ref[some, :] = lax.dot_general(
            cols_ref[:, some], final[...], (((0,), (0,)), ((), ())),
            preferred_element_type=jnp.float32,
        ).astype(jnp.bfloat16)

    gx.drain()
    gs.drain()
    for r in range(len(SPLIT)):
        for k in range(1, n):
            cols_copy((me + k) % n, me, r).wait_send()
    pl.when(bulk)(lambda: core_sum.wait_send())

    @pl.when(sums)
    def _():
        core_spread.wait_send()
        for k in range(1, chips):
            scatter(k, chip_at(k), chip).wait_send()
            spread(chip_at(k), chip).wait_send()


def exchange(n, x, f, g, of):
    sh, din = x.shape
    feat = f.shape[0]
    tokens, chips = n * sh, n // 2
    width, slab = g.shape[1] // n, of.shape[1]
    size = tokens // BLOCKS
    packed = PACKED * size
    bf, f32, dma = jnp.bfloat16, jnp.float32, pltpu.SemaphoreType.DMA
    scratch = [
        ((tokens, din), bf), (f.shape, bf), (g.shape, bf), ((tokens, width), bf),
        ((tokens, feat), bf), ((tokens, feat), bf),
        ((packed, size), f32), ((packed, size), f32), ((packed, size), bf),
        ((chips, packed // chips, size), bf), ((packed, size), bf), ((tokens, tokens), bf),
    ]
    used = sum(functools.reduce(lambda a, b: a * b, s) * jnp.dtype(t).itemsize for s, t in scratch)
    return pl.pallas_call(
        functools.partial(exchange_kernel, n),
        out_shape=(
            pltpu.VMEM(of.shape, of.dtype), pltpu.VMEM((tokens, slab), bf), pltpu.VMEM((width, tokens), bf),
        ),
        in_specs=[pl.BlockSpec(memory_space=pltpu.HBM)] * 4,
        out_specs=(pl.BlockSpec(memory_space=pltpu.VMEM),) * 3,
        scratch_shapes=[pltpu.VMEM(s, t) for s, t in scratch] + [
            dma((6,)), dma((n, 4)), dma((4, n)), dma((n, 2)), dma((4, n)),
            dma((len(SPLIT), n)), dma((len(SPLIT), n)), dma((2,)), dma((2,)),
            dma((chips,)), dma((chips,)), dma((chips,)), dma((chips,)),
        ],
        compiler_params=pltpu.CompilerParams(
            collective_id=0, has_side_effects=True, vmem_limit_bytes=used + 3 * 1024 * 1024
        ),
    )(*(pltpu.with_memory_space_constraint(v, pltpu.HBM) for v in (x, f, g, of)))


def write_kernel(upd, slab_ref, left, dst, buf, sem):
    tokens, slab = slab_ref.shape
    slots, high, strip = buf.shape
    down = upd.shape[0] // high
    blocks = down * (slab // strip)

    def place(j):
        return pl.ds(j % down * high, high), pl.ds(j // down * strip, strip)

    def copy(j):
        return pltpu.make_async_copy(buf.at[j % slots], dst.at[place(j)], sem.at[j % slots])

    for j in range(blocks):
        rs, cs = place(j)
        if j >= slots:
            copy(j - slots).wait()
        buf[j % slots] = upd[rs, cs] + jnp.dot(
            left[rs, :], slab_ref[:, cs], preferred_element_type=jnp.float32
        ) * (1.0 / tokens)
        copy(j).start()
    for j in range(max(0, blocks - slots), blocks):
        copy(j).wait()


def write(upd, slab_ref, left):
    strip = min(STRIP, upd.shape[1])
    slots = min(upd.shape[1] // strip, 4)
    return pl.pallas_call(
        write_kernel,
        out_shape=jax.ShapeDtypeStruct(upd.shape, upd.dtype),
        in_specs=[pl.BlockSpec(memory_space=pltpu.VMEM)] * 3,
        out_specs=pl.BlockSpec(memory_space=pl.ANY),
        scratch_shapes=[
            pltpu.VMEM((slots, upd.shape[0] // 2, strip), upd.dtype), pltpu.SemaphoreType.DMA((slots,)),
        ],
        compiler_params=pltpu.CompilerParams(vmem_limit_bytes=slots * upd.shape[0] * strip * 2 + 2 * 1024 * 1024),
    )(upd, slab_ref, left)


def per_device(n, inputs, input_factor, out_grads, output_factor):
    return write(*exchange(n, inputs, input_factor, out_grads, output_factor))


def solution(mesh):
    spec = P(("groups", "row"), None)
    return jax.shard_map(
        functools.partial(per_device, mesh.shape["row"]),
        mesh=mesh, in_specs=(spec,) * 4, out_specs=spec, check_vma=False,
    )
```
